512 devices in a mesh: ctx: 32 (over x, y), head: 16 (over z, core).
Axes of the slice: x: 4, y: 8, z: 8, core: 2. Of those that a mesh axis runs over, the one named last changes fastest.
Arguments:
- queries: bfloat16 [8192, 4096], P('ctx', 'head'), may hold values from -6 to 6
- keys_values: bfloat16 [8192, 1024], P('ctx'), may hold values from -6 to 6
- grad_rows: bfloat16 [8192, 2880], P('ctx', 'head'), may hold values from -6 to 6
- doc_ids: int32 [8192], replicated, may hold values from 0 to 7, never falling along the last dimension, each value on 1 to 2048 neighbouring positions
- tile_list: int32 [64], replicated, may hold values from 0 to 63, each once
Outputs:
- attended: float32 [8192, 4096], P('ctx', 'head')
- weight_grad: float32 [2880, 4096], P('ctx', 'head')
The draws below stay inside these ranges and needn't reach their ends.
Inputs may be any that keep to these rules, and one draw needn't show every extreme that they name: `tile_list`: every slot index names a different tile. `doc_ids`: never falling along the window; each document holds 1 to 2048 positions.
All inputs are finite; a program needn't handle non-finite values.
Results may differ from the reference program's by a relative error of at most 0.0018.
Values may be sent and summed in bfloat16 or wider, within the bound.
No kernel may reach another device: no remote copies, remote signals or barrier semaphores. Data moves between devices by JAX's collectives and lax.ppermute only.
A program may use at most 128 MiB of HBM per device.

```python
import math
import jax
import jax.numpy as jnp
import numpy as np
from jax import lax

D = 2880
H = 64
KVH = 8
DH = 64
TILE = 128
TOKENS = 8192


def draw_queries(key, part):
    base = jnp.clip(1.5 * jax.random.normal(jax.random.fold_in(key, 1), (TOKENS, H * DH), jnp.float32), -6.0, 6.0)
    return base.astype(jnp.bfloat16)


def draw_keys_values(key, part):
    base = jnp.clip(jax.random.normal(jax.random.fold_in(key, 4), (TOKENS, KVH, 2, DH), jnp.float32), -6.0, 6.0)
    return base.reshape(TOKENS, KVH * 2 * DH).astype(jnp.bfloat16)


def strengthened(values, key, source, target, shards_of, factor):
    def block_of(position):
        return (jnp.arange(values.shape[position]) // (values.shape[position] // shards_of)).reshape((-1,) + (1,) * (values.ndim - 1 - position))

    one_side = jax.random.permutation(key, shards_of)[block_of(target)]
    far = (block_of(target) + shards_of // 2) % shards_of
    return jnp.where((block_of(source) == one_side) | (block_of(source) == far), factor * values, values)


def shard_levels(key, extent, pieces, least, high):
    def one(dim, blocks):
        steps = jax.random.uniform(jax.random.fold_in(jax.random.fold_in(key, 6), dim), (blocks,), jnp.float32, least / len(pieces), high / len(pieces))
        return jnp.repeat(jnp.exp(steps), extent[dim] // blocks).reshape((-1,) + (1,) * (len(extent) - dim - 1))

    gain = one(*pieces[0])
    for cut in pieces[1:]:
        gain = gain * one(*cut)
    return gain


def split_up(number_of, total, bound, slope):
    portions = [(1 << 20) // math.isqrt(standing ** slope) + 1 for standing in range(2, number_of + 1)]
    rest, counts = total - bound - (number_of - 1), [1] * (number_of - 1)
    while rest > 0:
        free = [i for i in range(number_of - 1) if counts[i] < bound]
        whole, remaining = sum([portions[i] for i in free]), rest
        for i in free:
            more = min(bound - counts[i], max(1, remaining * portions[i] // whole), rest)
            counts[i] = counts[i] + more
            rest = rest - more
    return np.array([bound] + counts)


def ragged(own_key, amount, total, bound, lean):
    if amount == 2:
        one = jax.random.randint(own_key, (), max(1, total - bound), min(bound, total - 1) + 1)
        return jnp.stack([one, total - one])
    tallies = jnp.asarray(split_up(amount, total, bound, lean), jnp.int32)
    couples = (amount - 1) // 2
    donor, receiver = tallies[1:1 + 2 * couples:2], tallies[2:2 + 2 * couples:2]
    margin = jnp.minimum(donor - 1, bound - receiver)
    moved = jax.random.randint(jax.random.fold_in(own_key, 1), (couples,), 0, 1 << 20) % (margin + 1)
    tallies = tallies.at[1:1 + 2 * couples:2].set(donor - moved).at[2:2 + 2 * couples:2].set(receiver + moved)
    return tallies[jax.random.permutation(jax.random.fold_in(own_key, 2), amount)]


def noise_with(own_key, dims, deviation, bound, pieces, heavy, kind=jnp.bfloat16):
    drawn = deviation * jax.random.normal(own_key, dims, jnp.float32)
    if pieces:
        drawn = drawn * shard_levels(own_key, dims, pieces, -0.22, 0.18)
    return jnp.clip(strengthened(drawn, jax.random.fold_in(own_key, 3), *heavy), -bound, bound).astype(kind)


def setup_inputs(seed: int = 0) -> dict:
    key_of = jax.random.split(jax.random.key(seed), 6)
    queries = draw_queries(jax.random.fold_in(key_of[5], 71), 0)
    keys_values = draw_keys_values(jax.random.fold_in(key_of[5], 71), 0)
    grad_rows = noise_with(key_of[2], (TOKENS, D), 1.0, 6.0, ((0, 32), (1, 16)), (0, 1, 32, 2.75))
    doc_ids = jnp.searchsorted(jnp.cumsum(ragged(key_of[3], 8, TOKENS, TOKENS // 4, 1)), jnp.arange(TOKENS), side="right").astype(jnp.int32)
    tile_list = jax.random.permutation(key_of[4], TOKENS // TILE).astype(jnp.int32)
    return dict(queries=queries, keys_values=keys_values, grad_rows=grad_rows, doc_ids=doc_ids, tile_list=tile_list)


NEG_FILL = -1e30


def reference(queries, keys_values, grad_rows, doc_ids, tile_list):
    total = queries.shape[0]
    group = H // KVH
    scale = DH ** -0.5
    offsets = jnp.arange(TILE, dtype=jnp.int32)
    slot_pos = (tile_list[:, None] * TILE + offsets[None, :]).reshape(-1).astype(jnp.int32)
    slot_doc = doc_ids.reshape(-1, TILE)[tile_list].reshape(-1)
    blocks = keys_values.reshape(total, KVH, 2, DH).astype(jnp.float32)
    keys = blocks[:, :, 0]
    values = blocks[:, :, 1]
    grouped = queries.reshape(total, KVH, group, DH)
    rows = math.gcd(512, total)
    count = total // rows

    def one_block(index):
        start = (index * rows).astype(jnp.int32)
        query_pos = lax.dynamic_slice_in_dim(slot_pos, start, rows)
        query_doc = lax.dynamic_slice_in_dim(slot_doc, start, rows)
        allowed = (query_doc[:, None] == slot_doc[None, :]) & (slot_pos[None, :] <= query_pos[:, None])
        query_block = lax.dynamic_slice_in_dim(grouped, start, rows).astype(jnp.float32)

        def one_head(kv_head):
            query_head = query_block[:, kv_head]
            scores = jnp.einsum("tqd,nd->qtn", query_head, keys[:, kv_head]) * scale
            masked = jnp.where(allowed[None], scores, NEG_FILL)
            top = jnp.max(masked, axis=-1, keepdims=True)
            weights = jnp.where(allowed[None], jnp.exp(masked - top), 0.0)
            denom = jnp.sum(weights, axis=-1)
            rounded = lax.optimization_barrier(weights.astype(jnp.bfloat16)).astype(jnp.float32)
            summed = jnp.einsum("qtn,nd->tqd", rounded, values[:, kv_head])
            return summed / jnp.transpose(denom)[..., None]

        heads_out = lax.map(one_head, jnp.arange(KVH, dtype=jnp.int32))
        return jnp.transpose(heads_out, (1, 0, 2, 3)).reshape(rows, H * DH)

    attended = lax.map(one_block, jnp.arange(count, dtype=jnp.int32)).reshape(total, H * DH)
    weight_grad = jnp.dot(grad_rows.astype(jnp.float32).T, attended,
                          precision=lax.Precision.HIGHEST, preferred_element_type=jnp.float32)
    return attended, weight_grad
```

```python
import jax
import jax.numpy as jnp
from jax import lax
from jax.experimental import pallas as pl
from jax.experimental.pallas import tpu as pltpu
from jax.sharding import Mesh, PartitionSpec as P

H = 64
KVH = 8
DH = 64
TILE = 128
DOCS = 8
HEADS = 4
SPAN = 18
BLOCK = 90
PADDED = 96
NEG_FILL = -1e30


def attention_kernel(core_ref, tiles_ref, docs_ref, q_ref, own_ref, other_ref, out_ref, slot_ref, s_ref):
    count = tiles_ref.shape[0]
    tokens = docs_ref.shape[0]
    core = core_ref[0]
    first_slot = core_ref[1]
    width = HEADS * TILE

    def invert(slot, carry):
        slot_ref[tiles_ref[slot]] = slot
        return carry

    lax.fori_loop(0, count, invert, 0)

    def bisect(step, lows):
        size = lax.shift_right_logical(tokens, step + 1)
        return tuple(
            jnp.where(docs_ref[low + size - 1] < doc + 1, low + size, low) for doc, low in enumerate(lows)
        )

    steps = tokens.bit_length() - 1
    bounds = lax.fori_loop(0, steps, bisect, (jnp.int32(0),) * (DOCS - 1))
    bounds = tuple(
        jnp.where(docs_ref[jnp.minimum(low, tokens - 1)] < doc + 1, low + 1, low) for doc, low in enumerate(bounds)
    )

    lane = lax.broadcasted_iota(jnp.int32, (1, TILE), 1)
    sub = lax.broadcasted_iota(jnp.int32, (2 * TILE, TILE), 0)

    def pick(tile):
        slot = slot_ref[tile]
        at = lax.shift_right_logical(slot, 1)
        return jnp.where((slot & 1) == core, own_ref[at], other_ref[at])

    for part in range(2):
        tile = tiles_ref[first_slot + part]
        base = tile * TILE
        begin = jnp.int32(0)
        row_pos = base + lane
        row_begin = jnp.zeros((1, TILE), jnp.int32)
        for bound in bounds:
            begin = jnp.where(bound <= base, jnp.maximum(begin, bound), begin)
            row_begin = jnp.where(bound <= row_pos, jnp.maximum(row_begin, bound), row_begin)
        low = lax.div(begin, TILE)
        pairs = lax.div(tile - low + 2, 2)

        q = q_ref[part * TILE:(part + 1) * TILE, :]
        q_t = jnp.transpose(q.astype(jnp.float32) * (DH ** -0.5)).astype(jnp.bfloat16)
        q_t = jnp.concatenate([q_t[h * DH:(h + 1) * DH] for h in range(HEADS)], axis=1)
        q_t = jnp.concatenate([q_t, jnp.zeros_like(q_t)], axis=0)

        def score(pair, top):
            at = low + 2 * pair
            kv = jnp.concatenate([pick(at), pick(jnp.minimum(at + 1, tile))], axis=0)
            scores = jnp.dot(kv, q_t, preferred_element_type=jnp.float32)
            key_pos = at * TILE + sub
            allowed = (key_pos >= row_begin) & (key_pos <= row_pos)
            start = pl.multiple_of(pair * (2 * TILE), 2 * TILE)
            tops = []
            for h in range(HEADS):
                masked = jnp.where(allowed, scores[:, h * TILE:(h + 1) * TILE], NEG_FILL)
                s_ref[pl.ds(start, 2 * TILE), h * TILE:(h + 1) * TILE] = masked
                tops.append(jnp.max(masked.reshape(2 * TILE // 8, 8, TILE), axis=0))
            return jnp.maximum(top, jnp.concatenate(tops, axis=1))

        top = lax.fori_loop(0, pairs, score, jnp.full((8, width), NEG_FILL, jnp.float32))
        top = jnp.max(top, axis=0, keepdims=True)

        def add(pair, carry):
            total, summed = carry
            at = low + 2 * pair
            kv = jnp.concatenate([pick(at), pick(jnp.minimum(at + 1, tile))], axis=0)
            start = pl.multiple_of(pair * (2 * TILE), 2 * TILE)
            weights = jnp.exp(s_ref[pl.ds(start, 2 * TILE), :] - top)
            total = total + jnp.sum(weights.reshape(2 * TILE // 8, 8, width), axis=0)
            summed = summed + lax.dot_general(
                kv, weights.astype(jnp.bfloat16), (((0,), (0,)), ((), ())), preferred_element_type=jnp.float32
            )
            return total, summed

        total, summed = lax.fori_loop(
            0, pairs, add, (jnp.zeros((8, width), jnp.float32), jnp.zeros((2 * DH, width), jnp.float32))
        )
        total = jnp.sum(total, axis=0, keepdims=True)
        normed = summed[DH:] / total
        for h in range(0, HEADS, 2):
            both = jnp.concatenate(
                [normed[:, h * TILE:(h + 1) * TILE], normed[:, (h + 1) * TILE:(h + 2) * TILE]], axis=0
            )
            out_ref[part * TILE:(part + 1) * TILE, h * DH:(h + 2) * DH] = jnp.transpose(both)


def attention(core, tiles, docs, queries, own, other):
    smem = pl.BlockSpec(memory_space=pltpu.SMEM)
    vmem = pl.BlockSpec(memory_space=pltpu.VMEM)
    return pl.pallas_call(
        attention_kernel,
        out_shape=jax.ShapeDtypeStruct(queries.shape, jnp.float32),
        in_specs=[smem, smem, smem, vmem, vmem, vmem],
        out_specs=vmem,
        scratch_shapes=[
            pltpu.SMEM((tiles.shape[0],), jnp.int32),
            pltpu.VMEM((SPAN * TILE, HEADS * TILE), jnp.float32),
        ],
        cost_estimate=pl.CostEstimate(flops=1_200_000_000, bytes_accessed=4_000_000, transcendentals=2_200_000),
        compiler_params=pltpu.CompilerParams(vmem_limit_bytes=32 << 20),
    )(core, tiles, docs, queries, own, other)


def term_kernel(g_ref, a_ref, out_ref):
    a = a_ref[...]
    high = a.astype(jnp.bfloat16)
    low = (a - high.astype(jnp.float32)).astype(jnp.bfloat16)

    def step(i, carry):
        rows = pl.ds(pl.multiple_of(i * (4 * PADDED), 4 * PADDED), 4 * PADDED)
        g = g_ref[rows, :]
        term = jnp.dot(g, high, preferred_element_type=jnp.float32)
        term = term + jnp.dot(g, low, preferred_element_type=jnp.float32)
        out_ref[rows, :] = term.astype(out_ref.dtype)
        return carry

    lax.fori_loop(0, g_ref.shape[0] // (4 * PADDED), step, 0)


def term_of(grads, attended):
    vmem = pl.BlockSpec(memory_space=pltpu.VMEM)
    return pl.pallas_call(
        term_kernel,
        out_shape=jax.ShapeDtypeStruct((grads.shape[0], attended.shape[1]), jnp.bfloat16),
        in_specs=[vmem, vmem],
        out_specs=vmem,
        cost_estimate=pl.CostEstimate(flops=800_000_000, bytes_accessed=4_000_000, transcendentals=0),
        compiler_params=pltpu.CompilerParams(vmem_limit_bytes=32 << 20),
    )(grads, attended)


def everyone(x, axes, size):
    return lax.all_to_all(jnp.broadcast_to(x[None], (size,) + x.shape), axes, 0, 0)


def on_device(queries, keys_values, grad_rows, doc_ids, tile_list):
    nx, ny, nz, nc = (lax.axis_size(a) for a in ("x", "y", "z", "core"))
    core = lax.axis_index("core")
    ctx = lax.axis_index("x") * ny + lax.axis_index("y")
    tokens = queries.shape[0]

    mine = lax.dynamic_slice(keys_values, (core * TILE, lax.axis_index("z") * (2 * DH)), (TILE, 2 * DH))
    grads = jnp.pad(jnp.transpose(grad_rows).reshape(2, BLOCK, tokens), ((0, 0), (0, PADDED - BLOCK), (0, 0)))
    grads = everyone(grads, ("z", "core"), nz * nc).reshape(nz * nc * 2 * PADDED, tokens)

    own = everyone(mine, "y", ny)
    own = everyone(own, "x", nx).reshape(nx * ny, TILE, 2 * DH)
    other = lax.ppermute(own, "core", [(0, 1), (1, 0)])

    attended = attention(jnp.stack([core, 2 * ctx]), tile_list, doc_ids, queries, own, other)
    term = term_of(grads, attended).reshape(nx * ny, PADDED, attended.shape[1])
    parts = lax.all_to_all(term, ("x", "y"), 0, 0)
    weight_grad = jnp.sum(parts.astype(jnp.float32), axis=0)[:BLOCK]
    return attended, weight_grad


def solution(mesh):
    fine = Mesh(mesh.devices.reshape(4, 8, 8, 2), ("x", "y", "z", "core"))
    ctx, head = ("x", "y"), ("z", "core")
    in_specs = (P(ctx, head), P(ctx, None), P(ctx, head), P(), P())
    out_specs = (P(ctx, head), P(ctx, head))
    return jax.shard_map(on_device, mesh=fine, in_specs=in_specs, out_specs=out_specs, check_vma=False)
```

```python
import jax
import jax.numpy as jnp
from jax import lax
from jax.experimental import pallas as pl
from jax.experimental.pallas import tpu as pltpu
from jax.sharding import Mesh, PartitionSpec as P


DH = 64
TILE = 128
DOCS = 8
HEADS = 4
SPAN = 18
BLOCK = 90
PADDED = 96
NEG_FILL = -1e30


def attention_kernel(core_ref, tiles_ref, docs_ref, q_ref, own_ref, other_ref, out_ref, send_ref, slot_ref, s_ref):
    count = tiles_ref.shape[0]
    tokens = docs_ref.shape[0]
    core = core_ref[0]
    first_slot = core_ref[1]
    width = HEADS * TILE

    def invert(slot, carry):
        slot_ref[tiles_ref[slot]] = slot
        return carry

    lax.fori_loop(0, count, invert, 0)

    def bisect(step, lows):
        size = lax.shift_right_logical(tokens, step + 1)
        return tuple(
            jnp.where(docs_ref[low + size - 1] < doc + 1, low + size, low) for doc, low in enumerate(lows)
        )

    steps = tokens.bit_length() - 1
    bounds = lax.fori_loop(0, steps, bisect, (jnp.int32(0),) * (DOCS - 1))
    bounds = tuple(
        jnp.where(docs_ref[jnp.minimum(low, tokens - 1)] < doc + 1, low + 1, low) for doc, low in enumerate(bounds)
    )

    lane = lax.broadcasted_iota(jnp.int32, (1, TILE), 1)
    sub = lax.broadcasted_iota(jnp.int32, (2 * TILE, TILE), 0)

    def pick(tile):
        slot = slot_ref[tile]
        at = lax.shift_right_logical(slot, 1)
        return jnp.where((slot & 1) == core, own_ref[at], other_ref[at])

    for part in range(2):
        tile = tiles_ref[first_slot + part]
        base = tile * TILE
        begin = jnp.int32(0)
        row_pos = base + lane
        row_begin = jnp.zeros((1, TILE), jnp.int32)
        for bound in bounds:
            begin = jnp.where(bound <= base, jnp.maximum(begin, bound), begin)
            row_begin = jnp.where(bound <= row_pos, jnp.maximum(row_begin, bound), row_begin)
        low = lax.div(begin, TILE)
        pairs = lax.div(tile - low + 2, 2)

        q = q_ref[part * TILE:(part + 1) * TILE, :]
        q_t = jnp.transpose(q.astype(jnp.float32) * (DH ** -0.5)).astype(jnp.bfloat16)
        q_t = jnp.concatenate([q_t[h * DH:(h + 1) * DH] for h in range(HEADS)], axis=1)
        q_t = jnp.concatenate([q_t, jnp.zeros_like(q_t)], axis=0)

        def score(pair, top):
            at = low + 2 * pair
            kv = jnp.concatenate([pick(at), pick(jnp.minimum(at + 1, tile))], axis=0)
            scores = jnp.dot(kv, q_t, preferred_element_type=jnp.float32)
            key_pos = at * TILE + sub
            allowed = (key_pos >= row_begin) & (key_pos <= row_pos)
            start = pl.multiple_of(pair * (2 * TILE), 2 * TILE)
            tops = []
            for h in range(HEADS):
                masked = jnp.where(allowed, scores[:, h * TILE:(h + 1) * TILE], NEG_FILL)
                s_ref[pl.ds(start, 2 * TILE), h * TILE:(h + 1) * TILE] = masked
                tops.append(jnp.max(masked.reshape(2 * TILE // 8, 8, TILE), axis=0))
            return jnp.maximum(top, jnp.concatenate(tops, axis=1))

        top = lax.fori_loop(0, pairs, score, jnp.full((8, width), NEG_FILL, jnp.float32))
        top = jnp.max(top, axis=0, keepdims=True)

        def add(pair, carry):
            total, summed = carry
            at = low + 2 * pair
            kv = jnp.concatenate([pick(at), pick(jnp.minimum(at + 1, tile))], axis=0)
            start = pl.multiple_of(pair * (2 * TILE), 2 * TILE)
            weights = jnp.exp(s_ref[pl.ds(start, 2 * TILE), :] - top)
            total = total + jnp.sum(weights.reshape(2 * TILE // 8, 8, width), axis=0)
            summed = summed + lax.dot_general(
                kv, weights.astype(jnp.bfloat16), (((0,), (0,)), ((), ())), preferred_element_type=jnp.float32
            )
            return total, summed

        total, summed = lax.fori_loop(
            0, pairs, add, (jnp.zeros((8, width), jnp.float32), jnp.zeros((2 * DH, width), jnp.float32))
        )
        total = jnp.sum(total, axis=0, keepdims=True)
        normed = summed[DH:] / total
        for h in range(0, HEADS, 2):
            both = jnp.concatenate(
                [normed[:, h * TILE:(h + 1) * TILE], normed[:, (h + 1) * TILE:(h + 2) * TILE]], axis=0
            )
            both = jnp.transpose(both)
            out_ref[part * TILE:(part + 1) * TILE, h * DH:(h + 2) * DH] = both
            for peer in range(send_ref.shape[0]):
                send_ref[peer, part * TILE:(part + 1) * TILE, h * DH:(h + 2) * DH] = both.astype(send_ref.dtype)


def attention(core, tiles, docs, queries, own, other, peers):
    smem = pl.BlockSpec(memory_space=pltpu.SMEM)
    vmem = pl.BlockSpec(memory_space=pltpu.VMEM)
    return pl.pallas_call(
        attention_kernel,
        out_shape=(
            jax.ShapeDtypeStruct(queries.shape, jnp.float32),
            jax.ShapeDtypeStruct((peers,) + queries.shape, jnp.bfloat16),
        ),
        in_specs=[smem, smem, smem, vmem, vmem, vmem],
        out_specs=(vmem, vmem),
        scratch_shapes=[
            pltpu.SMEM((tiles.shape[0],), jnp.int32),
            pltpu.VMEM((SPAN * TILE, HEADS * TILE), jnp.float32),
        ],
        cost_estimate=pl.CostEstimate(flops=1_200_000_000, bytes_accessed=4_000_000, transcendentals=2_200_000),
        compiler_params=pltpu.CompilerParams(vmem_limit_bytes=32 << 20),
    )(core, tiles, docs, queries, own, other)


def term_kernel(place_ref, g_own_ref, g_other_ref, a_ref, own_ref, out_ref):
    core, x = place_ref[0], place_ref[1]
    pairs = out_ref.shape[0] // 2
    a = own_ref[...]
    low = (a - a.astype(jnp.bfloat16).astype(jnp.float32)).astype(jnp.bfloat16)
    for pair in range(pairs):
        for g_ref, side in ((g_own_ref, core), (g_other_ref, 1 - core)):
            term = jnp.dot(g_ref[pairs * x + pair], low, preferred_element_type=jnp.float32)
            for peer in range(a_ref.shape[0]):
                term = term + jnp.dot(
                    g_ref[pairs * peer + pair], a_ref[peer], preferred_element_type=jnp.float32
                )
            out_ref[2 * pair + side] = term


def term_of(place, g_own, g_other, gathered, attended):
    smem = pl.BlockSpec(memory_space=pltpu.SMEM)
    vmem = pl.BlockSpec(memory_space=pltpu.VMEM)
    blocks = 2 * g_own.shape[0] // gathered.shape[0]
    return pl.pallas_call(
        term_kernel,
        out_shape=jax.ShapeDtypeStruct((blocks, g_own.shape[1], attended.shape[1]), jnp.float32),
        in_specs=[smem, vmem, vmem, vmem, vmem],
        out_specs=vmem,
        cost_estimate=pl.CostEstimate(flops=500_000_000, bytes_accessed=3_000_000, transcendentals=0),
        compiler_params=pltpu.CompilerParams(vmem_limit_bytes=32 << 20),
    )(place, g_own, g_other, gathered, attended)


def everyone(x, axes, size):
    return lax.all_to_all(jnp.broadcast_to(x[None], (size,) + x.shape), axes, 0, 0)


def on_device(queries, keys_values, grad_rows, doc_ids, tile_list):
    nx, ny, nz = (lax.axis_size(a) for a in ("x", "y", "z"))
    core, x = lax.axis_index("core"), lax.axis_index("x")
    ctx = x * ny + lax.axis_index("y")
    tokens = queries.shape[0]
    swap = [(0, 1), (1, 0)]
    half = nz // nx

    grads = jnp.pad(jnp.transpose(grad_rows).reshape(2, BLOCK, tokens), ((0, 0), (0, PADDED - BLOCK), (0, 0)))
    grads = grads.reshape(2 * PADDED, tokens)
    turn = [(a * nz + half * b + c, b * nz + half * a + c) for a in range(nx) for b in range(nx) for c in range(half)]
    grads = lax.ppermute(grads, ("x", "z"), turn)

    mine = lax.dynamic_slice(keys_values, (core * TILE, lax.axis_index("z") * (2 * DH)), (TILE, 2 * DH))
    own = everyone(mine, "y", ny)
    own = everyone(own, "x", nx).reshape(nx * ny, TILE, 2 * DH)
    other = lax.ppermute(own, "core", swap)

    g_own = everyone(grads, "z", nz)
    g_other = lax.ppermute(g_own, "core", swap)

    attended, send = attention(
        jnp.stack([core, 2 * ctx]), tile_list, doc_ids, queries, own, other, nx
    )
    gathered = lax.all_to_all(send, "x", 0, 0)
    term = term_of(jnp.stack([core, x]), g_own, g_other, gathered, attended)
    parts = lax.all_to_all(term.reshape(ny, PADDED, attended.shape[1]), "y", 0, 0)
    weight_grad = jnp.sum(parts, axis=0)[:BLOCK]
    return attended, weight_grad


def solution(mesh):
    fine = Mesh(mesh.devices.reshape(4, 8, 8, 2), ("x", "y", "z", "core"))
    ctx, head = ("x", "y"), ("z", "core")
    in_specs = (P(ctx, head), P(ctx, None), P(ctx, head), P(), P())
    out_specs = (P(ctx, head), P(ctx, head))
    return jax.shard_map(on_device, mesh=fine, in_specs=in_specs, out_specs=out_specs, check_vma=False)
```

```python
import jax
import jax.numpy as jnp
from jax import lax
from jax.experimental import pallas as pl
from jax.experimental.pallas import tpu as pltpu
from jax.sharding import Mesh, PartitionSpec as P


DH = 64
TILE = 128
DOCS = 8
HEADS = 4
SPAN = 18
BLOCK = 90
PADDED = 96
NEG_FILL = -1e30


def attention_kernel(core_ref, tiles_ref, docs_ref, q_ref, own_ref, other_ref, out_ref, send_ref, slot_ref, s_ref):
    count = tiles_ref.shape[0]
    tokens = docs_ref.shape[0]
    core = core_ref[0]
    first_slot = core_ref[1]
    width = HEADS * TILE

    def invert(slot, carry):
        slot_ref[tiles_ref[slot]] = slot
        return carry

    lax.fori_loop(0, count, invert, 0)

    def bisect(step, lows):
        size = lax.shift_right_logical(tokens, step + 1)
        return tuple(
            jnp.where(docs_ref[low + size - 1] < doc + 1, low + size, low) for doc, low in enumerate(lows)
        )

    steps = tokens.bit_length() - 1
    bounds = lax.fori_loop(0, steps, bisect, (jnp.int32(0),) * (DOCS - 1))
    bounds = tuple(
        jnp.where(docs_ref[jnp.minimum(low, tokens - 1)] < doc + 1, low + 1, low) for doc, low in enumerate(bounds)
    )

    lane = lax.broadcasted_iota(jnp.int32, (1, TILE), 1)
    sub = lax.broadcasted_iota(jnp.int32, (2 * TILE, TILE), 0)

    def pick(tile):
        slot = slot_ref[tile]
        at = lax.shift_right_logical(slot, 1)
        return jnp.where((slot & 1) == core, own_ref[at], other_ref[at])

    for part in range(2):
        tile = tiles_ref[first_slot + part]
        base = tile * TILE
        begin = jnp.int32(0)
        row_pos = base + lane
        row_begin = jnp.zeros((1, TILE), jnp.int32)
        for bound in bounds:
            begin = jnp.where(bound <= base, jnp.maximum(begin, bound), begin)
            row_begin = jnp.where(bound <= row_pos, jnp.maximum(row_begin, bound), row_begin)
        low = lax.div(begin, TILE)
        pairs = lax.div(tile - low + 2, 2)

        q = q_ref[part * TILE:(part + 1) * TILE, :]
        q_t = jnp.transpose(q.astype(jnp.float32) * (DH ** -0.5)).astype(jnp.bfloat16)
        q_t = jnp.concatenate([q_t[h * DH:(h + 1) * DH] for h in range(HEADS)], axis=1)
        q_t = jnp.concatenate([q_t, jnp.zeros_like(q_t)], axis=0)

        def score(pair, top):
            at = low + 2 * pair
            kv = jnp.concatenate([pick(at), pick(jnp.minimum(at + 1, tile))], axis=0)
            scores = jnp.dot(kv, q_t, preferred_element_type=jnp.float32)
            key_pos = at * TILE + sub
            allowed = (key_pos >= row_begin) & (key_pos <= row_pos)
            start = pl.multiple_of(pair * (2 * TILE), 2 * TILE)
            tops = []
            for h in range(HEADS):
                masked = jnp.where(allowed, scores[:, h * TILE:(h + 1) * TILE], NEG_FILL)
                s_ref[pl.ds(start, 2 * TILE), h * TILE:(h + 1) * TILE] = masked
                tops.append(jnp.max(masked.reshape(2 * TILE // 8, 8, TILE), axis=0))
            return jnp.maximum(top, jnp.concatenate(tops, axis=1))

        top = lax.fori_loop(0, pairs, score, jnp.full((8, width), NEG_FILL, jnp.float32))
        top = jnp.max(top, axis=0, keepdims=True)

        def add(pair, carry):
            total, summed = carry
            at = low + 2 * pair
            kv = jnp.concatenate([pick(at), pick(jnp.minimum(at + 1, tile))], axis=0)
            start = pl.multiple_of(pair * (2 * TILE), 2 * TILE)
            weights = jnp.exp(s_ref[pl.ds(start, 2 * TILE), :] - top)
            total = total + jnp.sum(weights.reshape(2 * TILE // 8, 8, width), axis=0)
            summed = summed + lax.dot_general(
                kv, weights.astype(jnp.bfloat16), (((0,), (0,)), ((), ())), preferred_element_type=jnp.float32
            )
            return total, summed

        total, summed = lax.fori_loop(
            0, pairs, add, (jnp.zeros((8, width), jnp.float32), jnp.zeros((2 * DH, width), jnp.float32))
        )
        total = jnp.sum(total, axis=0, keepdims=True)
        normed = summed[DH:] / total
        for h in range(0, HEADS, 2):
            both = jnp.concatenate(
                [normed[:, h * TILE:(h + 1) * TILE], normed[:, (h + 1) * TILE:(h + 2) * TILE]], axis=0
            )
            both = jnp.transpose(both)
            out_ref[part * TILE:(part + 1) * TILE, h * DH:(h + 2) * DH] = both
            for peer in range(send_ref.shape[0]):
                send_ref[peer, part * TILE:(part + 1) * TILE, h * DH:(h + 2) * DH] = both.astype(send_ref.dtype)


def attention(core, tiles, docs, queries, own, other, peers):
    smem = pl.BlockSpec(memory_space=pltpu.SMEM)
    vmem = pl.BlockSpec(memory_space=pltpu.VMEM)
    return pl.pallas_call(
        attention_kernel,
        out_shape=(
            jax.ShapeDtypeStruct(queries.shape, jnp.float32),
            jax.ShapeDtypeStruct((peers,) + queries.shape, jnp.bfloat16),
        ),
        in_specs=[smem, smem, smem, vmem, vmem, vmem],
        out_specs=(vmem, vmem),
        scratch_shapes=[
            pltpu.SMEM((tiles.shape[0],), jnp.int32),
            pltpu.VMEM((SPAN * TILE, HEADS * TILE), jnp.float32),
        ],
        cost_estimate=pl.CostEstimate(flops=1_200_000_000, bytes_accessed=4_000_000, transcendentals=2_200_000),
        compiler_params=pltpu.CompilerParams(vmem_limit_bytes=32 << 20),
    )(core, tiles, docs, queries, own, other)


def term_kernel(place_ref, g_own_ref, g_other_ref, a_ref, own_ref, out_ref):
    core, x, z = place_ref[0], place_ref[1], place_ref[2]
    pairs = out_ref.shape[0] // 2

    def slot(peer, pair):
        apart = z ^ (pairs * peer + pair)
        return ((apart & 1) << 2) | (apart & 2) | (apart >> 2)

    a = own_ref[...]
    low = (a - a.astype(jnp.bfloat16).astype(jnp.float32)).astype(jnp.bfloat16)
    for pair in range(pairs):
        for g_ref, side in ((g_own_ref, core), (g_other_ref, 1 - core)):
            term = jnp.dot(g_ref[slot(x, pair)], low, preferred_element_type=jnp.float32)
            for peer in range(a_ref.shape[0]):
                term = term + jnp.dot(
                    g_ref[slot(peer, pair)], a_ref[peer], preferred_element_type=jnp.float32
                )
            out_ref[2 * pair + side] = term


def term_of(place, g_own, g_other, gathered, attended):
    smem = pl.BlockSpec(memory_space=pltpu.SMEM)
    vmem = pl.BlockSpec(memory_space=pltpu.VMEM)
    blocks = 2 * g_own.shape[0] // gathered.shape[0]
    return pl.pallas_call(
        term_kernel,
        out_shape=jax.ShapeDtypeStruct((blocks, g_own.shape[1], attended.shape[1]), jnp.float32),
        in_specs=[smem, vmem, vmem, vmem, vmem],
        out_specs=vmem,
        cost_estimate=pl.CostEstimate(flops=500_000_000, bytes_accessed=3_000_000, transcendentals=0),
        compiler_params=pltpu.CompilerParams(vmem_limit_bytes=32 << 20),
    )(place, g_own, g_other, gathered, attended)


def everyone(x, axes, size):
    return lax.all_to_all(jnp.broadcast_to(x[None], (size,) + x.shape), axes, 0, 0)


def on_device(queries, keys_values, grad_rows, doc_ids, tile_list):
    nx, ny, nz = (lax.axis_size(a) for a in ("x", "y", "z"))
    core, x = lax.axis_index("core"), lax.axis_index("x")
    ctx = x * ny + lax.axis_index("y")
    tokens = queries.shape[0]
    swap = [(0, 1), (1, 0)]
    half = nz // nx

    grads = jnp.pad(jnp.transpose(grad_rows).reshape(2, BLOCK, tokens), ((0, 0), (0, PADDED - BLOCK), (0, 0)))
    grads = grads.reshape(2 * PADDED, tokens)
    turn = [(a * nz + half * b + c, b * nz + half * a + c) for a in range(nx) for b in range(nx) for c in range(half)]
    grads = lax.ppermute(grads, ("x", "z"), turn)

    mine = lax.dynamic_slice(keys_values, (core * TILE, lax.axis_index("z") * (2 * DH)), (TILE, 2 * DH))
    own = everyone(mine, "y", ny)
    own = everyone(own, "x", nx).reshape(nx * ny, TILE, 2 * DH)
    other = lax.ppermute(own, "core", swap)

    g_own = grads[None]
    bit = nz // 2
    while bit:
        came = lax.ppermute(g_own, "z", [(i, i ^ bit) for i in range(nz)])
        g_own = jnp.concatenate([g_own, came], axis=0)
        bit //= 2
    g_other = lax.ppermute(g_own, "core", swap)

    attended, send = attention(
        jnp.stack([core, 2 * ctx]), tile_list, doc_ids, queries, own, other, nx
    )
    gathered = lax.all_to_all(send, "x", 0, 0)
    place = jnp.stack([core, x, lax.axis_index("z")])
    term = term_of(place, g_own, g_other, gathered, attended)
    parts = lax.all_to_all(term.reshape(ny, PADDED, attended.shape[1]), "y", 0, 0)
    weight_grad = jnp.sum(parts, axis=0)[:BLOCK]
    return attended, weight_grad


def solution(mesh):
    fine = Mesh(mesh.devices.reshape(4, 8, 8, 2), ("x", "y", "z", "core"))
    ctx, head = ("x", "y"), ("z", "core")
    in_specs = (P(ctx, head), P(ctx, None), P(ctx, head), P(), P())
    out_specs = (P(ctx, head), P(ctx, head))
    return jax.shard_map(on_device, mesh=fine, in_specs=in_specs, out_specs=out_specs, check_vma=False)
```

```python
import jax
import jax.numpy as jnp
from jax import lax
from jax.experimental import pallas as pl
from jax.experimental.pallas import tpu as pltpu
from jax.sharding import Mesh, PartitionSpec as P


DH = 64
TILE = 128
DOCS = 8
HEADS = 4
SPAN = 18
BLOCK = 90
PADDED = 96
NEG_FILL = -1e30


def tables_kernel(place_ref, tiles_ref, docs_ref, q_ref, table_ref, q_t_ref):
    count = tiles_ref.shape[0]
    tokens = docs_ref.shape[0]

    def invert(slot, carry):
        table_ref[tiles_ref[slot]] = slot
        return carry

    lax.fori_loop(0, count, invert, 0)

    def bisect(step, lows):
        size = lax.shift_right_logical(tokens, step + 1)
        return tuple(
            jnp.where(docs_ref[low + size - 1] < doc + 1, low + size, low) for doc, low in enumerate(lows)
        )

    steps = tokens.bit_length() - 1
    bounds = lax.fori_loop(0, steps, bisect, (jnp.int32(0),) * (DOCS - 1))
    for doc, low in enumerate(bounds):
        last = docs_ref[jnp.minimum(low, tokens - 1)] < doc + 1
        table_ref[count + doc] = jnp.where(last, low + 1, low)
    for part in range(2):
        table_ref[count + DOCS - 1 + part] = tiles_ref[place_ref[1] + part]
        q = q_ref[part * TILE:(part + 1) * TILE, :]
        q_t = jnp.transpose(q.astype(jnp.float32) * (DH ** -0.5)).astype(jnp.bfloat16)
        q_t = jnp.concatenate([q_t[h * DH:(h + 1) * DH] for h in range(HEADS)], axis=1)
        q_t_ref[part] = jnp.concatenate([q_t, jnp.zeros_like(q_t)], axis=0)


def tables_of(place, tiles, docs, queries):
    smem = pl.BlockSpec(memory_space=pltpu.SMEM)
    vmem = pl.BlockSpec(memory_space=pltpu.VMEM)
    return pl.pallas_call(
        tables_kernel,
        out_shape=(
            jax.ShapeDtypeStruct((tiles.shape[0] + DOCS + 1,), jnp.int32),
            jax.ShapeDtypeStruct((2, 2 * DH, HEADS * TILE), jnp.bfloat16),
        ),
        in_specs=[smem, smem, smem, vmem],
        out_specs=(smem, vmem),
        cost_estimate=pl.CostEstimate(flops=1_000_000, bytes_accessed=500_000, transcendentals=0),
        compiler_params=pltpu.CompilerParams(vmem_limit_bytes=8 << 20),
    )(place, tiles, docs, queries)


def attention_kernel(place_ref, table_ref, q_ref, own_ref, other_ref, out_ref, send_ref, s_ref):
    count = table_ref.shape[0] - DOCS - 1
    core = place_ref[0]
    width = HEADS * TILE
    bounds = [table_ref[count + doc] for doc in range(DOCS - 1)]

    lane = lax.broadcasted_iota(jnp.int32, (1, TILE), 1)
    sub = lax.broadcasted_iota(jnp.int32, (2 * TILE, TILE), 0)

    def pick(tile):
        slot = table_ref[tile]
        at = lax.shift_right_logical(slot, 1)
        return jnp.where((slot & 1) == core, own_ref[at], other_ref[at])

    for part in range(2):
        tile = table_ref[count + DOCS - 1 + part]
        base = tile * TILE
        begin = jnp.int32(0)
        row_pos = base + lane
        row_begin = jnp.zeros((1, TILE), jnp.int32)
        for bound in bounds:
            begin = jnp.where(bound <= base, jnp.maximum(begin, bound), begin)
            row_begin = jnp.where(bound <= row_pos, jnp.maximum(row_begin, bound), row_begin)
        low = lax.div(begin, TILE)
        pairs = lax.div(tile - low + 2, 2)

        q_t = q_ref[part]

        def score(pair, top):
            at = low + 2 * pair
            kv = jnp.concatenate([pick(at), pick(jnp.minimum(at + 1, tile))], axis=0)
            scores = jnp.dot(kv, q_t, preferred_element_type=jnp.float32)
            key_pos = at * TILE + sub
            allowed = (key_pos >= row_begin) & (key_pos <= row_pos)
            start = pl.multiple_of(pair * (2 * TILE), 2 * TILE)
            tops = []
            for h in range(HEADS):
                masked = jnp.where(allowed, scores[:, h * TILE:(h + 1) * TILE], NEG_FILL)
                s_ref[pl.ds(start, 2 * TILE), h * TILE:(h + 1) * TILE] = masked
                tops.append(jnp.max(masked.reshape(2 * TILE // 8, 8, TILE), axis=0))
            return jnp.maximum(top, jnp.concatenate(tops, axis=1))

        top = lax.fori_loop(0, pairs, score, jnp.full((8, width), NEG_FILL, jnp.float32))
        top = jnp.max(top, axis=0, keepdims=True)

        def add(pair, carry):
            total, summed = carry
            at = low + 2 * pair
            kv = jnp.concatenate([pick(at), pick(jnp.minimum(at + 1, tile))], axis=0)
            start = pl.multiple_of(pair * (2 * TILE), 2 * TILE)
            weights = jnp.exp(s_ref[pl.ds(start, 2 * TILE), :] - top)
            total = total + jnp.sum(weights.reshape(2 * TILE // 8, 8, width), axis=0)
            summed = summed + lax.dot_general(
                kv[:, DH:], weights.astype(jnp.bfloat16), (((0,), (0,)), ((), ())), preferred_element_type=jnp.float32
            )
            return total, summed

        total, summed = lax.fori_loop(
            0, pairs, add, (jnp.zeros((8, width), jnp.float32), jnp.zeros((DH, width), jnp.float32))
        )
        total = jnp.sum(total, axis=0, keepdims=True)
        normed = summed / total
        for h in range(0, HEADS, 2):
            both = jnp.concatenate(
                [normed[:, h * TILE:(h + 1) * TILE], normed[:, (h + 1) * TILE:(h + 2) * TILE]], axis=0
            )
            both = jnp.transpose(both)
            out_ref[part * TILE:(part + 1) * TILE, h * DH:(h + 2) * DH] = both
            for peer in range(send_ref.shape[0]):
                send_ref[peer, part * TILE:(part + 1) * TILE, h * DH:(h + 2) * DH] = both


def attention(place, table, q_t, own, other, peers):
    smem = pl.BlockSpec(memory_space=pltpu.SMEM)
    vmem = pl.BlockSpec(memory_space=pltpu.VMEM)
    rows, columns = 2 * TILE, HEADS * DH
    return pl.pallas_call(
        attention_kernel,
        out_shape=(
            jax.ShapeDtypeStruct((rows, columns), jnp.float32),
            jax.ShapeDtypeStruct((peers, rows, columns), jnp.float32),
        ),
        in_specs=[smem, smem, vmem, vmem, vmem],
        out_specs=(vmem, vmem),
        scratch_shapes=[pltpu.VMEM((SPAN * TILE, HEADS * TILE), jnp.float32)],
        cost_estimate=pl.CostEstimate(flops=1_200_000_000, bytes_accessed=4_000_000, transcendentals=2_200_000),
        compiler_params=pltpu.CompilerParams(vmem_limit_bytes=32 << 20),
    )(place, table, q_t, own, other)


def term_kernel(place_ref, g00_ref, g01_ref, g10_ref, g11_ref, a_ref, out_ref, own_ref, high_ref, low_ref, sum_ref):
    core, z, y = place_ref[0], place_ref[1], place_ref[2]
    a = a_ref[...]
    high = a.astype(jnp.bfloat16)
    high_ref[...] = high
    low_ref[...] = (a - high.astype(jnp.float32)).astype(jnp.bfloat16)
    for flip, sides in enumerate(((g00_ref, g01_ref), (g10_ref, g11_ref))):
        pair = (z & 1) ^ flip
        for side, g_ref in zip((core, 1 - core), sides, strict=True):
            term = None
            for i in range(g_ref.shape[0]):
                peer = lax.shift_right_logical(z, 1) ^ (((i & 1) << 1) | (i >> 1))
                for half_ref in (high_ref, low_ref):
                    part = jnp.dot(g_ref[i], half_ref[peer], preferred_element_type=jnp.float32)
                    term = part if term is None else term + part
            sum_ref[2 * pair + side] = term
            out_ref[2 * pair + side] = term.astype(out_ref.dtype)
    own_ref[...] = sum_ref[lax.shift_right_logical(y, 1), pl.ds(pl.multiple_of((y & 1) * PADDED, PADDED), PADDED), :]


def term_of(place, grads, gathered):
    smem = pl.BlockSpec(memory_space=pltpu.SMEM)
    vmem = pl.BlockSpec(memory_space=pltpu.VMEM)
    blocks, rows = grads[0].shape[0], grads[0].shape[1]
    columns = gathered.shape[2]
    return pl.pallas_call(
        term_kernel,
        out_shape=(
            jax.ShapeDtypeStruct((blocks, rows, columns), jnp.bfloat16),
            jax.ShapeDtypeStruct((PADDED, columns), jnp.float32),
        ),
        in_specs=[smem] + [vmem] * 5,
        out_specs=(vmem, vmem),
        scratch_shapes=[
            pltpu.VMEM(gathered.shape, jnp.bfloat16),
            pltpu.VMEM(gathered.shape, jnp.bfloat16),
            pltpu.VMEM((blocks, rows, columns), jnp.float32),
        ],
        cost_estimate=pl.CostEstimate(flops=900_000_000, bytes_accessed=3_000_000, transcendentals=0),
        compiler_params=pltpu.CompilerParams(vmem_limit_bytes=32 << 20),
    )(place, *grads, gathered)


def everyone(x, axes, size):
    return lax.all_to_all(jnp.broadcast_to(x[None], (size,) + x.shape), axes, 0, 0)


def on_device(queries, keys_values, grad_rows, doc_ids, tile_list):
    nx, ny, nz = (lax.axis_size(a) for a in ("x", "y", "z"))
    core, x = lax.axis_index("core"), lax.axis_index("x")
    ctx = x * ny + lax.axis_index("y")
    tokens = queries.shape[0]
    swap = [(0, 1), (1, 0)]
    half = nz // nx

    grads = jnp.pad(jnp.transpose(grad_rows).reshape(2, BLOCK, tokens), ((0, 0), (0, PADDED - BLOCK), (0, 0)))
    grads = grads.reshape(2 * PADDED, tokens)
    turn = [(a * nz + half * b + c, b * nz + half * a + c) for a in range(nx) for b in range(nx) for c in range(half)]
    grads = lax.ppermute(grads, ("x", "z"), turn)

    mine = lax.dynamic_slice(keys_values, (core * TILE, lax.axis_index("z") * (2 * DH)), (TILE, 2 * DH))
    own = everyone(mine, "y", ny)
    own = everyone(own, "x", nx).reshape(nx * ny, TILE, 2 * DH)
    other = lax.ppermute(own, "core", swap)

    place = jnp.stack([core, 2 * ctx])
    table, q_t = tables_of(place, tile_list, doc_ids, queries)

    g_own = grads[None]
    for bit in (4, 2):
        came = lax.ppermute(g_own, "z", [(i, i ^ bit) for i in range(nz)])
        g_own = jnp.concatenate([g_own, came], axis=0)
    g_next = lax.ppermute(g_own, "z", [(i, i ^ 1) for i in range(nz)])
    g_other = lax.ppermute(g_own, "core", swap)
    g_both = lax.ppermute(g_next, "core", swap)

    attended, send = attention(place, table, q_t, own, other, nx)
    gathered = lax.all_to_all(send, "x", 0, 0)
    y = lax.axis_index("y")
    place = jnp.stack([core, lax.axis_index("z"), y])
    term, mine = term_of(place, (g_own, g_other, g_next, g_both), gathered)
    parts = lax.all_to_all(term.reshape(ny, PADDED, -1), "y", 0, 0)
    others = lax.broadcasted_iota(jnp.int32, parts.shape, 0) != y
    weight_grad = (mine + jnp.sum(jnp.where(others, parts.astype(jnp.float32), 0.0), axis=0))[:BLOCK]
    return attended, weight_grad


def solution(mesh):
    fine = Mesh(mesh.devices.reshape(4, 8, 8, 2), ("x", "y", "z", "core"))
    ctx, head = ("x", "y"), ("z", "core")
    in_specs = (P(ctx, head), P(ctx, None), P(ctx, head), P(), P())
    out_specs = (P(ctx, head), P(ctx, head))
    return jax.shard_map(on_device, mesh=fine, in_specs=in_specs, out_specs=out_specs, check_vma=False)
```

```python
import jax
import jax.numpy as jnp
from jax import lax
from jax.experimental import pallas as pl
from jax.experimental.pallas import tpu as pltpu
from jax.sharding import Mesh, PartitionSpec as P


DH = 64
TILE = 128
DOCS = 8
HEADS = 4
SPAN = 18
BLOCK = 90
PADDED = 96
NEG_FILL = -1e30


def tables_kernel(place_ref, tiles_ref, docs_ref, q_ref, table_ref, q_t_ref):
    count = tiles_ref.shape[0]
    tokens = docs_ref.shape[0]

    def invert(slot, carry):
        table_ref[tiles_ref[slot]] = slot
        return carry

    lax.fori_loop(0, count, invert, 0)

    def bisect(step, lows):
        size = lax.shift_right_logical(tokens, step + 1)
        return tuple(
            jnp.where(docs_ref[low + size - 1] < doc + 1, low + size, low) for doc, low in enumerate(lows)
        )

    steps = tokens.bit_length() - 1
    bounds = lax.fori_loop(0, steps, bisect, (jnp.int32(0),) * (DOCS - 1))
    for doc, low in enumerate(bounds):
        last = docs_ref[jnp.minimum(low, tokens - 1)] < doc + 1
        table_ref[count + doc] = jnp.where(last, low + 1, low)
    for part in range(2):
        table_ref[count + DOCS - 1 + part] = tiles_ref[place_ref[1] + part]
        q = q_ref[part * TILE:(part + 1) * TILE, :]
        q_t = jnp.transpose(q.astype(jnp.float32) * (DH ** -0.5)).astype(jnp.bfloat16)
        q_t = jnp.concatenate([q_t[h * DH:(h + 1) * DH] for h in range(HEADS)], axis=1)
        q_t_ref[part] = jnp.concatenate([q_t, jnp.zeros_like(q_t)], axis=0)


def tables_of(place, tiles, docs, queries):
    smem = pl.BlockSpec(memory_space=pltpu.SMEM)
    vmem = pl.BlockSpec(memory_space=pltpu.VMEM)
    return pl.pallas_call(
        tables_kernel,
        out_shape=(
            jax.ShapeDtypeStruct((tiles.shape[0] + DOCS + 1,), jnp.int32),
            jax.ShapeDtypeStruct((2, 2 * DH, HEADS * TILE), jnp.bfloat16),
        ),
        in_specs=[smem, smem, smem, vmem],
        out_specs=(smem, vmem),
        cost_estimate=pl.CostEstimate(flops=1_000_000, bytes_accessed=500_000, transcendentals=0),
        compiler_params=pltpu.CompilerParams(vmem_limit_bytes=8 << 20),
    )(place, tiles, docs, queries)


def attention_kernel(place_ref, table_ref, q_ref, own_ref, other_ref, out_ref, send_ref, s_ref, o_ref, b_ref, sems):
    count = table_ref.shape[0] - DOCS - 1
    core = place_ref[0]
    width = HEADS * TILE
    bounds = [table_ref[count + doc] for doc in range(DOCS - 1)]

    lane = lax.broadcasted_iota(jnp.int32, (1, TILE), 1)
    sub = lax.broadcasted_iota(jnp.int32, (2 * TILE, TILE), 0)

    def pick(tile):
        slot = table_ref[tile]
        at = lax.shift_right_logical(slot, 1)
        return jnp.where((slot & 1) == core, own_ref[at], other_ref[at])

    copies = []
    for part in range(2):
        tile = table_ref[count + DOCS - 1 + part]
        base = tile * TILE
        begin = jnp.int32(0)
        row_pos = base + lane
        row_begin = jnp.zeros((1, TILE), jnp.int32)
        for bound in bounds:
            begin = jnp.where(bound <= base, jnp.maximum(begin, bound), begin)
            row_begin = jnp.where(bound <= row_pos, jnp.maximum(row_begin, bound), row_begin)
        low = lax.div(begin, TILE)
        pairs = lax.div(tile - low + 2, 2)

        q_t = q_ref[part]

        def score(pair, top):
            at = low + 2 * pair
            kv = jnp.concatenate([pick(at), pick(jnp.minimum(at + 1, tile))], axis=0)
            scores = jnp.dot(kv, q_t, preferred_element_type=jnp.float32)
            key_pos = at * TILE + sub
            allowed = (key_pos >= row_begin) & (key_pos <= row_pos)
            start = pl.multiple_of(pair * (2 * TILE), 2 * TILE)
            tops = []
            for h in range(HEADS):
                masked = jnp.where(allowed, scores[:, h * TILE:(h + 1) * TILE], NEG_FILL)
                s_ref[pl.ds(start, 2 * TILE), h * TILE:(h + 1) * TILE] = masked
                tops.append(jnp.max(masked.reshape(2 * TILE // 8, 8, TILE), axis=0))
            return jnp.maximum(top, jnp.concatenate(tops, axis=1))

        top = lax.fori_loop(0, pairs, score, jnp.full((8, width), NEG_FILL, jnp.float32))
        top = jnp.max(top, axis=0, keepdims=True)

        def add(pair, carry):
            total, summed = carry
            at = low + 2 * pair
            kv = jnp.concatenate([pick(at), pick(jnp.minimum(at + 1, tile))], axis=0)
            start = pl.multiple_of(pair * (2 * TILE), 2 * TILE)
            weights = jnp.exp(s_ref[pl.ds(start, 2 * TILE), :] - top)
            total = total + jnp.sum(weights.reshape(2 * TILE // 8, 8, width), axis=0)
            summed = summed + lax.dot_general(
                kv[:, DH:], weights.astype(jnp.bfloat16), (((0,), (0,)), ((), ())), preferred_element_type=jnp.float32
            )
            return total, summed

        total, summed = lax.fori_loop(
            0, pairs, add, (jnp.zeros((8, width), jnp.float32), jnp.zeros((DH, width), jnp.float32))
        )
        total = jnp.sum(total, axis=0, keepdims=True)
        normed = summed / total
        for h in range(0, HEADS, 2):
            both = jnp.concatenate(
                [normed[:, h * TILE:(h + 1) * TILE], normed[:, (h + 1) * TILE:(h + 2) * TILE]], axis=0
            )
            both = jnp.transpose(both)
            o_ref[part, :, h * DH:(h + 2) * DH] = both
            b_ref[part, :, h * DH:(h + 2) * DH] = both.astype(b_ref.dtype)
        rows = pl.ds(part * TILE, TILE)
        copies.append(pltpu.make_async_copy(o_ref.at[part], out_ref.at[rows], sems.at[part, 0]))
        for peer in range(send_ref.shape[0]):
            copies.append(pltpu.make_async_copy(b_ref.at[part], send_ref.at[peer, rows], sems.at[part, 1 + peer]))
        for copy in copies[-1 - send_ref.shape[0]:]:
            copy.start()
    for copy in copies:
        copy.wait()


def attention(place, table, q_t, own, other, peers):
    smem = pl.BlockSpec(memory_space=pltpu.SMEM)
    vmem = pl.BlockSpec(memory_space=pltpu.VMEM)
    rows, columns = 2 * TILE, HEADS * DH
    return pl.pallas_call(
        attention_kernel,
        out_shape=(
            jax.ShapeDtypeStruct((rows, columns), jnp.float32),
            jax.ShapeDtypeStruct((peers, rows, columns), jnp.bfloat16),
        ),
        in_specs=[smem, smem, vmem, vmem, vmem],
        out_specs=(pl.BlockSpec(memory_space=pl.ANY), pl.BlockSpec(memory_space=pl.ANY)),
        scratch_shapes=[
            pltpu.VMEM((SPAN * TILE, HEADS * TILE), jnp.float32),
            pltpu.VMEM((2, TILE, columns), jnp.float32),
            pltpu.VMEM((2, TILE, columns), jnp.bfloat16),
            pltpu.SemaphoreType.DMA((2, 1 + peers)),
        ],
        cost_estimate=pl.CostEstimate(flops=1_200_000_000, bytes_accessed=4_000_000, transcendentals=2_200_000),
        compiler_params=pltpu.CompilerParams(vmem_limit_bytes=32 << 20),
    )(place, table, q_t, own, other)


def term_kernel(place_ref, g00_ref, g01_ref, g10_ref, g11_ref, a_ref, own_ref, out_ref):
    core, z, x = place_ref[0], place_ref[1], place_ref[2]
    zx = lax.shift_right_logical(z, 1)
    apart = zx ^ x
    at = ((apart & 1) << 1) | lax.shift_right_logical(apart, 1)
    a = own_ref[...]
    low = (a - a.astype(jnp.bfloat16).astype(jnp.float32)).astype(jnp.bfloat16)
    for flip, sides in enumerate(((g00_ref, g01_ref), (g10_ref, g11_ref))):
        pair = (z & 1) ^ flip
        for side, g_ref in zip((core, 1 - core), sides, strict=True):
            term = jnp.dot(g_ref[at], low, preferred_element_type=jnp.float32)
            for i in range(g_ref.shape[0]):
                peer = zx ^ (((i & 1) << 1) | (i >> 1))
                term = term + jnp.dot(g_ref[i], a_ref[peer], preferred_element_type=jnp.float32)
            out_ref[2 * pair + side] = term


def term_of(place, grads, gathered, attended):
    smem = pl.BlockSpec(memory_space=pltpu.SMEM)
    vmem = pl.BlockSpec(memory_space=pltpu.VMEM)
    blocks, rows = grads[0].shape[0], grads[0].shape[1]
    return pl.pallas_call(
        term_kernel,
        out_shape=jax.ShapeDtypeStruct((blocks, rows, attended.shape[1]), jnp.float32),
        in_specs=[smem] + [vmem] * 6,
        out_specs=vmem,
        cost_estimate=pl.CostEstimate(flops=500_000_000, bytes_accessed=3_000_000, transcendentals=0),
        compiler_params=pltpu.CompilerParams(vmem_limit_bytes=32 << 20),
    )(place, *grads, gathered, attended)


def everyone(x, axes, size):
    return lax.all_to_all(jnp.broadcast_to(x[None], (size,) + x.shape), axes, 0, 0)


def on_device(queries, keys_values, grad_rows, doc_ids, tile_list):
    nx, ny, nz = (lax.axis_size(a) for a in ("x", "y", "z"))
    core, x = lax.axis_index("core"), lax.axis_index("x")
    ctx = x * ny + lax.axis_index("y")
    tokens = queries.shape[0]
    swap = [(0, 1), (1, 0)]
    half = nz // nx

    grads = jnp.pad(jnp.transpose(grad_rows).reshape(2, BLOCK, tokens), ((0, 0), (0, PADDED - BLOCK), (0, 0)))
    grads = grads.reshape(2 * PADDED, tokens)
    turn = [(a * nz + half * b + c, b * nz + half * a + c) for a in range(nx) for b in range(nx) for c in range(half)]
    grads = lax.ppermute(grads, ("x", "z"), turn)

    mine = lax.dynamic_slice(keys_values, (core * TILE, lax.axis_index("z") * (2 * DH)), (TILE, 2 * DH))
    own = everyone(mine, "y", ny)
    own = everyone(own, "x", nx).reshape(nx * ny, TILE, 2 * DH)
    other = lax.ppermute(own, "core", swap)

    place = jnp.stack([core, 2 * ctx])
    table, q_t = tables_of(place, tile_list, doc_ids, queries)

    g_own = grads[None]
    for bit in (4, 2):
        came = lax.ppermute(g_own, "z", [(i, i ^ bit) for i in range(nz)])
        g_own = jnp.concatenate([g_own, came], axis=0)
    g_next = lax.ppermute(g_own, "z", [(i, i ^ 1) for i in range(nz)])
    g_other = lax.ppermute(g_own, "core", swap)
    g_both = lax.ppermute(g_next, "core", swap)

    attended, send = attention(place, table, q_t, own, other, nx)
    gathered = lax.all_to_all(send, "x", 0, 0)
    place = jnp.stack([core, lax.axis_index("z"), x])
    term = term_of(place, (g_own, g_other, g_next, g_both), gathered, attended)
    parts = lax.all_to_all(term.reshape(ny, PADDED, -1), "y", 0, 0)
    weight_grad = jnp.sum(parts, axis=0)[:BLOCK]
    return attended, weight_grad


def solution(mesh):
    fine = Mesh(mesh.devices.reshape(4, 8, 8, 2), ("x", "y", "z", "core"))
    ctx, head = ("x", "y"), ("z", "core")
    in_specs = (P(ctx, head), P(ctx, None), P(ctx, head), P(), P())
    out_specs = (P(ctx, head), P(ctx, head))
    return jax.shard_map(on_device, mesh=fine, in_specs=in_specs, out_specs=out_specs, check_vma=False)
```

```python
import jax
import jax.numpy as jnp
from jax import lax
from jax.experimental import pallas as pl
from jax.experimental.pallas import tpu as pltpu
from jax.sharding import Mesh, PartitionSpec as P


DH = 64
TILE = 128
DOCS = 8
HEADS = 4
SPAN = 18
BLOCK = 90
PADDED = 96
NEG_FILL = -1e30


def tables_kernel(place_ref, tiles_ref, docs_ref, q_ref, table_ref, q_t_ref):
    count = tiles_ref.shape[0]
    tokens = docs_ref.shape[0]

    def invert(slot, carry):
        table_ref[tiles_ref[slot]] = slot
        return carry

    lax.fori_loop(0, count, invert, 0)

    def bisect(step, lows):
        size = lax.shift_right_logical(tokens, step + 1)
        return tuple(
            jnp.where(docs_ref[low + size - 1] < doc + 1, low + size, low) for doc, low in enumerate(lows)
        )

    steps = tokens.bit_length() - 1
    bounds = lax.fori_loop(0, steps, bisect, (jnp.int32(0),) * (DOCS - 1))
    for doc, low in enumerate(bounds):
        last = docs_ref[jnp.minimum(low, tokens - 1)] < doc + 1
        table_ref[count + doc] = jnp.where(last, low + 1, low)
    for part in range(2):
        table_ref[count + DOCS - 1 + part] = tiles_ref[place_ref[1] + part]
        q = q_ref[part * TILE:(part + 1) * TILE, :]
        q_t = jnp.transpose(q.astype(jnp.float32) * (DH ** -0.5)).astype(jnp.bfloat16)
        q_t = jnp.concatenate([q_t[h * DH:(h + 1) * DH] for h in range(HEADS)], axis=1)
        q_t_ref[part] = jnp.concatenate([q_t, jnp.zeros_like(q_t)], axis=0)


def tables_of(place, tiles, docs, queries):
    smem = pl.BlockSpec(memory_space=pltpu.SMEM)
    vmem = pl.BlockSpec(memory_space=pltpu.VMEM)
    return pl.pallas_call(
        tables_kernel,
        out_shape=(
            jax.ShapeDtypeStruct((tiles.shape[0] + DOCS + 1,), jnp.int32),
            jax.ShapeDtypeStruct((2, 2 * DH, HEADS * TILE), jnp.bfloat16),
        ),
        in_specs=[smem, smem, smem, vmem],
        out_specs=(smem, vmem),
        cost_estimate=pl.CostEstimate(flops=1_000_000, bytes_accessed=500_000, transcendentals=0),
        compiler_params=pltpu.CompilerParams(vmem_limit_bytes=8 << 20),
    )(place, tiles, docs, queries)


def attention_kernel(place_ref, table_ref, q_ref, own_ref, other_ref, out_ref, send_ref, s_ref, o_ref, b_ref, sems):
    count = table_ref.shape[0] - DOCS - 1
    core = place_ref[0]
    width = HEADS * TILE
    bounds = [table_ref[count + doc] for doc in range(DOCS - 1)]

    lane = lax.broadcasted_iota(jnp.int32, (1, TILE), 1)
    sub = lax.broadcasted_iota(jnp.int32, (2 * TILE, TILE), 0)

    def pick(tile):
        slot = table_ref[tile]
        ctx = lax.shift_right_logical(slot, 1)
        y, x = lax.rem(ctx, own_ref.shape[0]), lax.div(ctx, own_ref.shape[0])
        return jnp.where((slot & 1) == core, own_ref[y, x], other_ref[y, x])

    copies = []
    for part in range(2):
        tile = table_ref[count + DOCS - 1 + part]
        base = tile * TILE
        begin = jnp.int32(0)
        row_pos = base + lane
        row_begin = jnp.zeros((1, TILE), jnp.int32)
        for bound in bounds:
            begin = jnp.where(bound <= base, jnp.maximum(begin, bound), begin)
            row_begin = jnp.where(bound <= row_pos, jnp.maximum(row_begin, bound), row_begin)
        low = lax.div(begin, TILE)
        pairs = lax.div(tile - low + 2, 2)

        q_t = q_ref[part]

        def score(pair, top):
            at = low + 2 * pair
            kv = jnp.concatenate([pick(at), pick(jnp.minimum(at + 1, tile))], axis=0)
            scores = jnp.dot(kv, q_t, preferred_element_type=jnp.float32)
            key_pos = at * TILE + sub
            allowed = (key_pos >= row_begin) & (key_pos <= row_pos)
            start = pl.multiple_of(pair * (2 * TILE), 2 * TILE)
            tops = []
            for h in range(HEADS):
                masked = jnp.where(allowed, scores[:, h * TILE:(h + 1) * TILE], NEG_FILL)
                s_ref[pl.ds(start, 2 * TILE), h * TILE:(h + 1) * TILE] = masked
                tops.append(jnp.max(masked.reshape(2 * TILE // 8, 8, TILE), axis=0))
            return jnp.maximum(top, jnp.concatenate(tops, axis=1))

        top = lax.fori_loop(0, pairs, score, jnp.full((8, width), NEG_FILL, jnp.float32))
        top = jnp.max(top, axis=0, keepdims=True)

        def add(pair, carry):
            total, summed = carry
            at = low + 2 * pair
            kv = jnp.concatenate([pick(at), pick(jnp.minimum(at + 1, tile))], axis=0)
            start = pl.multiple_of(pair * (2 * TILE), 2 * TILE)
            weights = jnp.exp(s_ref[pl.ds(start, 2 * TILE), :] - top)
            total = total + jnp.sum(weights.reshape(2 * TILE // 8, 8, width), axis=0)
            summed = summed + lax.dot_general(
                kv[:, DH:], weights.astype(jnp.bfloat16), (((0,), (0,)), ((), ())), preferred_element_type=jnp.float32
            )
            return total, summed

        total, summed = lax.fori_loop(
            0, pairs, add, (jnp.zeros((8, width), jnp.float32), jnp.zeros((DH, width), jnp.float32))
        )
        total = jnp.sum(total, axis=0, keepdims=True)
        normed = summed / total
        for h in range(0, HEADS, 2):
            both = jnp.concatenate(
                [normed[:, h * TILE:(h + 1) * TILE], normed[:, (h + 1) * TILE:(h + 2) * TILE]], axis=0
            )
            both = jnp.transpose(both)
            o_ref[part, :, h * DH:(h + 2) * DH] = both
            b_ref[part, :, h * DH:(h + 2) * DH] = both.astype(b_ref.dtype)
        rows = pl.ds(part * TILE, TILE)
        copies.append(pltpu.make_async_copy(o_ref.at[part], out_ref.at[rows], sems.at[part, 0]))
        for peer in range(send_ref.shape[0]):
            copies.append(pltpu.make_async_copy(b_ref.at[part], send_ref.at[peer, rows], sems.at[part, 1 + peer]))
        for copy in copies[-1 - send_ref.shape[0]:]:
            copy.start()
    for copy in copies:
        copy.wait()


def attention(place, table, q_t, own, other, peers):
    smem = pl.BlockSpec(memory_space=pltpu.SMEM)
    vmem = pl.BlockSpec(memory_space=pltpu.VMEM)
    rows, columns = 2 * TILE, HEADS * DH
    return pl.pallas_call(
        attention_kernel,
        out_shape=(
            jax.ShapeDtypeStruct((rows, columns), jnp.float32),
            jax.ShapeDtypeStruct((peers, rows, columns), jnp.bfloat16),
        ),
        in_specs=[smem, smem, vmem, vmem, vmem],
        out_specs=(pl.BlockSpec(memory_space=pl.ANY), pl.BlockSpec(memory_space=pl.ANY)),
        scratch_shapes=[
            pltpu.VMEM((SPAN * TILE, HEADS * TILE), jnp.float32),
            pltpu.VMEM((2, TILE, columns), jnp.float32),
            pltpu.VMEM((2, TILE, columns), jnp.bfloat16),
            pltpu.SemaphoreType.DMA((2, 1 + peers)),
        ],
        cost_estimate=pl.CostEstimate(flops=1_200_000_000, bytes_accessed=4_000_000, transcendentals=2_200_000),
        compiler_params=pltpu.CompilerParams(vmem_limit_bytes=32 << 20),
    )(place, table, q_t, own, other)


def term_kernel(place_ref, g00_ref, g01_ref, g10_ref, g11_ref, a_ref, own_ref, out_ref):
    core, z, x = place_ref[0], place_ref[1], place_ref[2]
    zx = lax.shift_right_logical(z, 1)
    apart = zx ^ x
    at = ((apart & 1) << 1) | lax.shift_right_logical(apart, 1)
    a = own_ref[...]
    low = (a - a.astype(jnp.bfloat16).astype(jnp.float32)).astype(jnp.bfloat16)
    for flip, sides in enumerate(((g00_ref, g01_ref), (g10_ref, g11_ref))):
        pair = (z & 1) ^ flip
        for side, g_ref in zip((core, 1 - core), sides, strict=True):
            term = jnp.dot(g_ref[at], low, preferred_element_type=jnp.float32)
            for i in range(g_ref.shape[0]):
                peer = zx ^ (((i & 1) << 1) | (i >> 1))
                term = term + jnp.dot(g_ref[i], a_ref[peer], preferred_element_type=jnp.float32)
            out_ref[2 * pair + side] = term


def term_of(place, grads, gathered, attended):
    smem = pl.BlockSpec(memory_space=pltpu.SMEM)
    vmem = pl.BlockSpec(memory_space=pltpu.VMEM)
    blocks, rows = grads[0].shape[0], grads[0].shape[1]
    return pl.pallas_call(
        term_kernel,
        out_shape=jax.ShapeDtypeStruct((blocks, rows, attended.shape[1]), jnp.float32),
        in_specs=[smem] + [vmem] * 6,
        out_specs=vmem,
        cost_estimate=pl.CostEstimate(flops=500_000_000, bytes_accessed=3_000_000, transcendentals=0),
        compiler_params=pltpu.CompilerParams(vmem_limit_bytes=32 << 20),
    )(place, *grads, gathered, attended)


def everyone(x, axes, size):
    return lax.all_to_all(jnp.broadcast_to(x[None], (size,) + x.shape), axes, 0, 0)


def on_device(queries, keys_values, grad_rows, doc_ids, tile_list):
    nx, ny, nz = (lax.axis_size(a) for a in ("x", "y", "z"))
    core, x = lax.axis_index("core"), lax.axis_index("x")
    ctx = x * ny + lax.axis_index("y")
    tokens = queries.shape[0]
    swap = [(0, 1), (1, 0)]
    half = nz // nx

    grads = jnp.pad(jnp.transpose(grad_rows).reshape(2, BLOCK, tokens), ((0, 0), (0, PADDED - BLOCK), (0, 0)))
    grads = grads.reshape(2 * PADDED, tokens)
    turn = [(a * nz + half * b + c, b * nz + half * a + c) for a in range(nx) for b in range(nx) for c in range(half)]
    grads = lax.ppermute(grads, ("x", "z"), turn)

    mine = lax.dynamic_slice(keys_values, (core * TILE, lax.axis_index("z") * (2 * DH)), (TILE, 2 * DH))
    own = everyone(mine, "x", nx)
    own = everyone(own, "y", ny)
    other = lax.ppermute(own, "core", swap)

    place = jnp.stack([core, 2 * ctx])
    table, q_t = tables_of(place, tile_list, doc_ids, queries)

    g_own = grads[None]
    for bit in (4, 2):
        came = lax.ppermute(g_own, "z", [(i, i ^ bit) for i in range(nz)])
        g_own = jnp.concatenate([g_own, came], axis=0)
    g_next = lax.ppermute(g_own, "z", [(i, i ^ 1) for i in range(nz)])
    g_other = lax.ppermute(g_own, "core", swap)
    g_both = lax.ppermute(g_next, "core", swap)

    attended, send = attention(place, table, q_t, own, other, nx)
    gathered = lax.all_to_all(send, "x", 0, 0)
    place = jnp.stack([core, lax.axis_index("z"), x])
    term = term_of(place, (g_own, g_other, g_next, g_both), gathered, attended)
    parts = lax.all_to_all(term.reshape(ny, PADDED, -1), "y", 0, 0)
    weight_grad = jnp.sum(parts, axis=0)[:BLOCK]
    return attended, weight_grad


def solution(mesh):
    fine = Mesh(mesh.devices.reshape(4, 8, 8, 2), ("x", "y", "z", "core"))
    ctx, head = ("x", "y"), ("z", "core")
    in_specs = (P(ctx, head), P(ctx, None), P(ctx, head), P(), P())
    out_specs = (P(ctx, head), P(ctx, head))
    return jax.shard_map(on_device, mesh=fine, in_specs=in_specs, out_specs=out_specs, check_vma=False)
```

```python
import jax
import jax.numpy as jnp
from jax import lax
from jax.experimental import pallas as pl
from jax.experimental.pallas import tpu as pltpu
from jax.sharding import Mesh, PartitionSpec as P


DH = 64
TILE = 128
DOCS = 8
HEADS = 4
SPAN = 18
BLOCK = 90
PADDED = 96
NEG_FILL = -1e30


def tables_kernel(place_ref, tiles_ref, docs_ref, q_ref, table_ref, q_t_ref):
    count = tiles_ref.shape[0]

    def invert(slot, carry):
        table_ref[tiles_ref[slot]] = slot
        return carry

    lax.fori_loop(0, count, invert, 0)

    docs = docs_ref[...]
    for doc in range(1, DOCS):
        before = jnp.sum(jnp.where(docs < doc, 1.0, 0.0))
        table_ref[count + doc - 1] = before.astype(jnp.int32)
    for part in range(2):
        table_ref[count + DOCS - 1 + part] = tiles_ref[place_ref[1] + part]
        q = q_ref[part * TILE:(part + 1) * TILE, :]
        q_t = jnp.transpose(q.astype(jnp.float32) * (DH ** -0.5)).astype(jnp.bfloat16)
        q_t = jnp.concatenate([q_t[h * DH:(h + 1) * DH] for h in range(HEADS)], axis=1)
        q_t_ref[part] = jnp.concatenate([q_t, jnp.zeros_like(q_t)], axis=0)


def tables_of(place, tiles, docs, queries):
    smem = pl.BlockSpec(memory_space=pltpu.SMEM)
    vmem = pl.BlockSpec(memory_space=pltpu.VMEM)
    return pl.pallas_call(
        tables_kernel,
        out_shape=(
            jax.ShapeDtypeStruct((tiles.shape[0] + DOCS + 1,), jnp.int32),
            jax.ShapeDtypeStruct((2, 2 * DH, HEADS * TILE), jnp.bfloat16),
        ),
        in_specs=[smem, smem, vmem, vmem],
        out_specs=(smem, vmem),
        cost_estimate=pl.CostEstimate(flops=1_000_000, bytes_accessed=500_000, transcendentals=0),
        compiler_params=pltpu.CompilerParams(vmem_limit_bytes=8 << 20),
    )(place, tiles, docs.reshape(-1, TILE), queries)


def attention_kernel(place_ref, table_ref, q_ref, own_ref, other_ref, out_ref, send_ref, s_ref, o_ref, sems):
    count = table_ref.shape[0] - DOCS - 1
    core = place_ref[0]
    width = HEADS * TILE
    bounds = [table_ref[count + doc] for doc in range(DOCS - 1)]

    lane = lax.broadcasted_iota(jnp.int32, (1, TILE), 1)
    sub = lax.broadcasted_iota(jnp.int32, (2 * TILE, TILE), 0)

    def pick(tile):
        slot = table_ref[tile]
        at = lax.shift_right_logical(slot, 1)
        return jnp.where((slot & 1) == core, own_ref[at], other_ref[at])

    copies = []
    for part in range(2):
        tile = table_ref[count + DOCS - 1 + part]
        base = tile * TILE
        begin = jnp.int32(0)
        row_pos = base + lane
        row_begin = jnp.zeros((1, TILE), jnp.int32)
        for bound in bounds:
            begin = jnp.where(bound <= base, jnp.maximum(begin, bound), begin)
            row_begin = jnp.where(bound <= row_pos, jnp.maximum(row_begin, bound), row_begin)
        low = lax.div(begin, TILE)
        pairs = lax.div(tile - low + 2, 2)

        q_t = q_ref[part]

        def score(pair, top):
            at = low + 2 * pair
            kv = jnp.concatenate([pick(at), pick(jnp.minimum(at + 1, tile))], axis=0)
            scores = jnp.dot(kv, q_t, preferred_element_type=jnp.float32)
            key_pos = at * TILE + sub
            allowed = (key_pos >= row_begin) & (key_pos <= row_pos)
            start = pl.multiple_of(pair * (2 * TILE), 2 * TILE)
            tops = []
            for h in range(HEADS):
                masked = jnp.where(allowed, scores[:, h * TILE:(h + 1) * TILE], NEG_FILL)
                s_ref[pl.ds(start, 2 * TILE), h * TILE:(h + 1) * TILE] = masked
                tops.append(jnp.max(masked.reshape(2 * TILE // 8, 8, TILE), axis=0))
            return jnp.maximum(top, jnp.concatenate(tops, axis=1))

        top = lax.fori_loop(0, pairs, score, jnp.full((8, width), NEG_FILL, jnp.float32))
        top = jnp.max(top, axis=0, keepdims=True)

        def add(pair, carry):
            total, summed = carry
            at = low + 2 * pair
            kv = jnp.concatenate([pick(at), pick(jnp.minimum(at + 1, tile))], axis=0)
            start = pl.multiple_of(pair * (2 * TILE), 2 * TILE)
            weights = jnp.exp(s_ref[pl.ds(start, 2 * TILE), :] - top)
            total = total + jnp.sum(weights.reshape(2 * TILE // 8, 8, width), axis=0)
            summed = summed + lax.dot_general(
                kv[:, DH:], weights.astype(jnp.bfloat16), (((0,), (0,)), ((), ())), preferred_element_type=jnp.float32
            )
            return total, summed

        total, summed = lax.fori_loop(
            0, pairs, add, (jnp.zeros((8, width), jnp.float32), jnp.zeros((DH, width), jnp.float32))
        )
        total = jnp.sum(total, axis=0, keepdims=True)
        normed = summed / total
        for h in range(0, HEADS, 2):
            both = jnp.concatenate(
                [normed[:, h * TILE:(h + 1) * TILE], normed[:, (h + 1) * TILE:(h + 2) * TILE]], axis=0
            )
            both = jnp.transpose(both)
            o_ref[part, :, h * DH:(h + 2) * DH] = both
        rows = pl.ds(part * TILE, TILE)
        copies.append(pltpu.make_async_copy(o_ref.at[part], out_ref.at[rows], sems.at[part, 0]))
        for peer in range(send_ref.shape[0]):
            copies.append(pltpu.make_async_copy(o_ref.at[part], send_ref.at[peer, rows], sems.at[part, 1 + peer]))
        for copy in copies[-1 - send_ref.shape[0]:]:
            copy.start()
    for copy in copies:
        copy.wait()


def attention(place, table, q_t, own, other, peers):
    smem = pl.BlockSpec(memory_space=pltpu.SMEM)
    vmem = pl.BlockSpec(memory_space=pltpu.VMEM)
    rows, columns = 2 * TILE, HEADS * DH
    return pl.pallas_call(
        attention_kernel,
        out_shape=(
            jax.ShapeDtypeStruct((rows, columns), jnp.float32),
            jax.ShapeDtypeStruct((peers, rows, columns), jnp.float32),
        ),
        in_specs=[smem, smem, vmem, vmem, vmem],
        out_specs=(pl.BlockSpec(memory_space=pl.ANY), pl.BlockSpec(memory_space=pl.ANY)),
        scratch_shapes=[
            pltpu.VMEM((SPAN * TILE, HEADS * TILE), jnp.float32),
            pltpu.VMEM((2, TILE, columns), jnp.float32),
            pltpu.SemaphoreType.DMA((2, 1 + peers)),
        ],
        cost_estimate=pl.CostEstimate(flops=1_200_000_000, bytes_accessed=4_000_000, transcendentals=2_200_000),
        compiler_params=pltpu.CompilerParams(vmem_limit_bytes=32 << 20),
    )(place, table, q_t, own, other)


def term_kernel(place_ref, g00_ref, g01_ref, g10_ref, g11_ref, a_ref, out_ref, own_ref, high_ref, low_ref, sum_ref):
    core, z, y = place_ref[0], place_ref[1], place_ref[2]
    a = a_ref[...]
    high = a.astype(jnp.bfloat16)
    high_ref[...] = high
    low_ref[...] = (a - high.astype(jnp.float32)).astype(jnp.bfloat16)
    places = ([z ^ k for k in (0, 4, 2, 6)], [(z + k) & 7 for k in (1, 5, 7, 3)])
    for flip, sides in enumerate(((g00_ref, g01_ref), (g10_ref, g11_ref))):
        pair = (z & 1) ^ flip
        for side, g_ref in zip((core, 1 - core), sides, strict=True):
            term = None
            for i, place in enumerate(places[flip]):
                peer = lax.shift_right_logical(place, 1)
                for half_ref in (high_ref, low_ref):
                    part = jnp.dot(g_ref[i], half_ref[peer], preferred_element_type=jnp.float32)
                    term = part if term is None else term + part
            sum_ref[2 * pair + side] = term
            out_ref[2 * pair + side] = term.astype(out_ref.dtype)
    own_ref[...] = sum_ref[lax.shift_right_logical(y, 1), pl.ds(pl.multiple_of((y & 1) * PADDED, PADDED), PADDED), :]


def term_of(place, grads, gathered):
    smem = pl.BlockSpec(memory_space=pltpu.SMEM)
    vmem = pl.BlockSpec(memory_space=pltpu.VMEM)
    blocks, rows = grads[0].shape[0], grads[0].shape[1]
    columns = gathered.shape[2]
    return pl.pallas_call(
        term_kernel,
        out_shape=(
            jax.ShapeDtypeStruct((blocks, rows, columns), jnp.bfloat16),
            jax.ShapeDtypeStruct((PADDED, columns), jnp.float32),
        ),
        in_specs=[smem] + [vmem] * 5,
        out_specs=(vmem, vmem),
        scratch_shapes=[
            pltpu.VMEM(gathered.shape, jnp.bfloat16),
            pltpu.VMEM(gathered.shape, jnp.bfloat16),
            pltpu.VMEM((blocks, rows, columns), jnp.float32),
        ],
        cost_estimate=pl.CostEstimate(flops=900_000_000, bytes_accessed=3_000_000, transcendentals=0),
        compiler_params=pltpu.CompilerParams(vmem_limit_bytes=32 << 20),
    )(place, *grads, gathered)


def everyone(x, axes, size):
    return lax.all_to_all(jnp.broadcast_to(x[None], (size,) + x.shape), axes, 0, 0)


def on_device(queries, keys_values, grad_rows, doc_ids, tile_list):
    nx, ny, nz = (lax.axis_size(a) for a in ("x", "y", "z"))
    core, x = lax.axis_index("core"), lax.axis_index("x")
    ctx = x * ny + lax.axis_index("y")
    tokens = queries.shape[0]
    swap = [(0, 1), (1, 0)]
    half = nz // nx

    grads = jnp.pad(jnp.transpose(grad_rows).reshape(2, BLOCK, tokens), ((0, 0), (0, PADDED - BLOCK), (0, 0)))
    grads = grads.reshape(2 * PADDED, tokens)
    turn = [(a * nz + half * b + c, b * nz + half * a + c) for a in range(nx) for b in range(nx) for c in range(half)]
    grads = lax.ppermute(grads, ("x", "z"), turn)

    mine = lax.dynamic_slice(keys_values, (core * TILE, lax.axis_index("z") * (2 * DH)), (TILE, 2 * DH))
    own = everyone(mine, "y", ny)
    own = everyone(own, "x", nx).reshape(nx * ny, TILE, 2 * DH)
    other = lax.ppermute(own, "core", swap)

    place = jnp.stack([core, 2 * ctx])
    table, q_t = tables_of(place, tile_list, doc_ids, queries)

    came = lax.ppermute(grads[None], "z", [(i, i ^ 4) for i in range(nz)])
    g_pair = jnp.concatenate([grads[None], came], axis=0)
    g_even = lax.ppermute(g_pair, "z", [(i, i ^ 2) for i in range(nz)])
    g_up = lax.ppermute(g_pair, "z", [((i + 1) % nz, i) for i in range(nz)])
    g_down = lax.ppermute(g_pair, "z", [(i, (i + 1) % nz) for i in range(nz)])
    g_own = jnp.concatenate([g_pair, g_even], axis=0)
    g_next = jnp.concatenate([g_up, g_down], axis=0)
    g_other = lax.ppermute(g_own, "core", swap)
    g_both = lax.ppermute(g_next, "core", swap)

    attended, send = attention(place, table, q_t, own, other, nx)
    gathered = lax.all_to_all(send, "x", 0, 0)
    y = lax.axis_index("y")
    place = jnp.stack([core, lax.axis_index("z"), y])
    term, mine = term_of(place, (g_own, g_other, g_next, g_both), gathered)
    parts = lax.all_to_all(term.reshape(ny, PADDED, -1), "y", 0, 0)
    others = lax.broadcasted_iota(jnp.int32, parts.shape, 0) != y
    weight_grad = (mine + jnp.sum(jnp.where(others, parts.astype(jnp.float32), 0.0), axis=0))[:BLOCK]
    return attended, weight_grad


def solution(mesh):
    fine = Mesh(mesh.devices.reshape(4, 8, 8, 2), ("x", "y", "z", "core"))
    ctx, head = ("x", "y"), ("z", "core")
    in_specs = (P(ctx, head), P(ctx, None), P(ctx, head), P(), P())
    out_specs = (P(ctx, head), P(ctx, head))
    return jax.shard_map(on_device, mesh=fine, in_specs=in_specs, out_specs=out_specs, check_vma=False)
```

```python
import jax
import jax.numpy as jnp
from jax import lax
from jax.experimental import pallas as pl
from jax.experimental.pallas import tpu as pltpu
from jax.sharding import Mesh, PartitionSpec as P


DH = 64
TILE = 128
DOCS = 8
HEADS = 4
SPAN = 18
BLOCK = 90
PADDED = 96
NEG_FILL = -1e30


def attention_kernel(
    place_ref, tiles_ref, docs_ref, q_ref, own_ref, other_ref, out_ref, send_ref, slot_ref, s_ref, o_ref, sems
):
    core = place_ref[0]
    width = HEADS * TILE

    for slot in range(tiles_ref.shape[0]):
        slot_ref[tiles_ref[slot]] = slot
    docs = docs_ref[...]
    bounds = [jnp.sum(jnp.where(docs < doc, 1.0, 0.0)).astype(jnp.int32) for doc in range(1, DOCS)]

    lane = lax.broadcasted_iota(jnp.int32, (1, TILE), 1)
    sub = lax.broadcasted_iota(jnp.int32, (2 * TILE, TILE), 0)

    def pick(tile):
        slot = slot_ref[tile]
        at = lax.shift_right_logical(slot, 1)
        return jnp.where((slot & 1) == core, own_ref[at], other_ref[at])

    copies = []
    for part in range(2):
        tile = tiles_ref[place_ref[1] + part]
        base = tile * TILE
        begin = jnp.int32(0)
        row_pos = base + lane
        row_begin = jnp.zeros((1, TILE), jnp.int32)
        for bound in bounds:
            begin = jnp.where(bound <= base, jnp.maximum(begin, bound), begin)
            row_begin = jnp.where(bound <= row_pos, jnp.maximum(row_begin, bound), row_begin)
        low = lax.div(begin, TILE)
        pairs = lax.div(tile - low + 2, 2)

        q = q_ref[part * TILE:(part + 1) * TILE, :]
        q_t = jnp.transpose(q.astype(jnp.float32) * (DH ** -0.5)).astype(jnp.bfloat16)
        q_t = jnp.concatenate([q_t[h * DH:(h + 1) * DH] for h in range(HEADS)], axis=1)
        q_t = jnp.concatenate([q_t, jnp.zeros_like(q_t)], axis=0)

        def score(pair, top):
            at = low + 2 * pair
            kv = jnp.concatenate([pick(at), pick(jnp.minimum(at + 1, tile))], axis=0)
            scores = jnp.dot(kv, q_t, preferred_element_type=jnp.float32)
            key_pos = at * TILE + sub
            allowed = (key_pos >= row_begin) & (key_pos <= row_pos)
            start = pl.multiple_of(pair * (2 * TILE), 2 * TILE)
            tops = []
            for h in range(HEADS):
                masked = jnp.where(allowed, scores[:, h * TILE:(h + 1) * TILE], NEG_FILL)
                s_ref[pl.ds(start, 2 * TILE), h * TILE:(h + 1) * TILE] = masked
                tops.append(jnp.max(masked.reshape(2 * TILE // 8, 8, TILE), axis=0))
            return jnp.maximum(top, jnp.concatenate(tops, axis=1))

        top = lax.fori_loop(0, pairs, score, jnp.full((8, width), NEG_FILL, jnp.float32))
        top = jnp.max(top, axis=0, keepdims=True)

        def add(pair, carry):
            total, summed = carry
            at = low + 2 * pair
            kv = jnp.concatenate([pick(at), pick(jnp.minimum(at + 1, tile))], axis=0)
            start = pl.multiple_of(pair * (2 * TILE), 2 * TILE)
            weights = jnp.exp(s_ref[pl.ds(start, 2 * TILE), :] - top)
            total = total + jnp.sum(weights.reshape(2 * TILE // 8, 8, width), axis=0)
            summed = summed + lax.dot_general(
                kv[:, DH:], weights.astype(jnp.bfloat16), (((0,), (0,)), ((), ())), preferred_element_type=jnp.float32
            )
            return total, summed

        total, summed = lax.fori_loop(
            0, pairs, add, (jnp.zeros((8, width), jnp.float32), jnp.zeros((DH, width), jnp.float32))
        )
        total = jnp.sum(total, axis=0, keepdims=True)
        normed = summed / total
        for h in range(0, HEADS, 2):
            both = jnp.concatenate(
                [normed[:, h * TILE:(h + 1) * TILE], normed[:, (h + 1) * TILE:(h + 2) * TILE]], axis=0
            )
            both = jnp.transpose(both)
            o_ref[part, :, h * DH:(h + 2) * DH] = both
        rows = pl.ds(part * TILE, TILE)
        copies.append(pltpu.make_async_copy(o_ref.at[part], out_ref.at[rows], sems.at[part, 0]))
        for peer in range(send_ref.shape[0]):
            copies.append(pltpu.make_async_copy(o_ref.at[part], send_ref.at[peer, rows], sems.at[part, 1 + peer]))
        for copy in copies[-1 - send_ref.shape[0]:]:
            copy.start()
    for copy in copies:
        copy.wait()


def attention(place, tiles, docs, queries, own, other, peers):
    smem = pl.BlockSpec(memory_space=pltpu.SMEM)
    vmem = pl.BlockSpec(memory_space=pltpu.VMEM)
    rows, columns = queries.shape
    return pl.pallas_call(
        attention_kernel,
        out_shape=(
            jax.ShapeDtypeStruct((rows, columns), jnp.float32),
            jax.ShapeDtypeStruct((peers, rows, columns), jnp.float32),
        ),
        in_specs=[smem, smem, vmem, vmem, vmem, vmem],
        out_specs=(pl.BlockSpec(memory_space=pl.ANY), pl.BlockSpec(memory_space=pl.ANY)),
        scratch_shapes=[
            pltpu.SMEM((tiles.shape[0],), jnp.int32),
            pltpu.VMEM((SPAN * TILE, HEADS * TILE), jnp.float32),
            pltpu.VMEM((2, TILE, columns), jnp.float32),
            pltpu.SemaphoreType.DMA((2, 1 + peers)),
        ],
        cost_estimate=pl.CostEstimate(flops=1_200_000_000, bytes_accessed=4_000_000, transcendentals=2_200_000),
        compiler_params=pltpu.CompilerParams(vmem_limit_bytes=32 << 20),
    )(place, tiles, docs.reshape(-1, TILE), queries, own, other)


def term_kernel(place_ref, g00_ref, g01_ref, g10_ref, g11_ref, a_ref, out_ref, own_ref, high_ref, low_ref, sum_ref):
    core, z, y = place_ref[0], place_ref[1], place_ref[2]
    a = a_ref[...]
    high = a.astype(jnp.bfloat16)
    high_ref[...] = high
    low_ref[...] = (a - high.astype(jnp.float32)).astype(jnp.bfloat16)
    for flip, sides in enumerate(((g00_ref, g01_ref), (g10_ref, g11_ref))):
        pair = (z & 1) ^ flip
        for side, g_ref in zip((core, 1 - core), sides, strict=True):
            term = None
            for i in range(g_ref.shape[0]):
                peer = lax.shift_right_logical(z, 1) ^ (((i & 1) << 1) | (i >> 1))
                for half_ref in (high_ref, low_ref):
                    part = jnp.dot(g_ref[i], half_ref[peer], preferred_element_type=jnp.float32)
                    term = part if term is None else term + part
            sum_ref[2 * pair + side] = term
            out_ref[2 * pair + side] = term.astype(out_ref.dtype)
    own_ref[...] = sum_ref[lax.shift_right_logical(y, 1), pl.ds(pl.multiple_of((y & 1) * PADDED, PADDED), PADDED), :]


def term_of(place, grads, gathered):
    smem = pl.BlockSpec(memory_space=pltpu.SMEM)
    vmem = pl.BlockSpec(memory_space=pltpu.VMEM)
    blocks, rows = grads[0].shape[0], grads[0].shape[1]
    columns = gathered.shape[2]
    return pl.pallas_call(
        term_kernel,
        out_shape=(
            jax.ShapeDtypeStruct((blocks, rows, columns), jnp.bfloat16),
            jax.ShapeDtypeStruct((PADDED, columns), jnp.float32),
        ),
        in_specs=[smem] + [vmem] * 5,
        out_specs=(vmem, vmem),
        scratch_shapes=[
            pltpu.VMEM(gathered.shape, jnp.bfloat16),
            pltpu.VMEM(gathered.shape, jnp.bfloat16),
            pltpu.VMEM((blocks, rows, columns), jnp.float32),
        ],
        cost_estimate=pl.CostEstimate(flops=900_000_000, bytes_accessed=3_000_000, transcendentals=0),
        compiler_params=pltpu.CompilerParams(vmem_limit_bytes=32 << 20),
    )(place, *grads, gathered)


def everyone(x, axes, size):
    return lax.all_to_all(jnp.broadcast_to(x[None], (size,) + x.shape), axes, 0, 0)


def on_device(queries, keys_values, grad_rows, doc_ids, tile_list):
    nx, ny, nz = (lax.axis_size(a) for a in ("x", "y", "z"))
    core, x = lax.axis_index("core"), lax.axis_index("x")
    ctx = x * ny + lax.axis_index("y")
    tokens = queries.shape[0]
    swap = [(0, 1), (1, 0)]
    half = nz // nx

    grads = jnp.pad(jnp.transpose(grad_rows).reshape(2, BLOCK, tokens), ((0, 0), (0, PADDED - BLOCK), (0, 0)))
    grads = grads.reshape(2 * PADDED, tokens)
    turn = [(a * nz + half * b + c, b * nz + half * a + c) for a in range(nx) for b in range(nx) for c in range(half)]
    grads = lax.ppermute(grads, ("x", "z"), turn)

    mine = lax.dynamic_slice(keys_values, (core * TILE, lax.axis_index("z") * (2 * DH)), (TILE, 2 * DH))
    own = everyone(mine, "y", ny)
    own = everyone(own, "x", nx).reshape(nx * ny, TILE, 2 * DH)
    other = lax.ppermute(own, "core", swap)

    g_own = grads[None]
    for bit in (4, 2):
        came = lax.ppermute(g_own, "z", [(i, i ^ bit) for i in range(nz)])
        g_own = jnp.concatenate([g_own, came], axis=0)
    g_next = lax.ppermute(g_own, "z", [(i, i ^ 1) for i in range(nz)])
    g_other = lax.ppermute(g_own, "core", swap)
    g_both = lax.ppermute(g_next, "core", swap)

    place = jnp.stack([core, 2 * ctx])
    attended, send = attention(place, tile_list, doc_ids, queries, own, other, nx)
    gathered = lax.all_to_all(send, "x", 0, 0)
    y = lax.axis_index("y")
    place = jnp.stack([core, lax.axis_index("z"), y])
    term, mine = term_of(place, (g_own, g_other, g_next, g_both), gathered)
    parts = lax.all_to_all(term.reshape(ny, PADDED, -1), "y", 0, 0)
    others = lax.broadcasted_iota(jnp.int32, parts.shape, 0) != y
    weight_grad = (mine + jnp.sum(jnp.where(others, parts.astype(jnp.float32), 0.0), axis=0))[:BLOCK]
    return attended, weight_grad


def solution(mesh):
    fine = Mesh(mesh.devices.reshape(4, 8, 8, 2), ("x", "y", "z", "core"))
    ctx, head = ("x", "y"), ("z", "core")
    in_specs = (P(ctx, head), P(ctx, None), P(ctx, head), P(), P())
    out_specs = (P(ctx, head), P(ctx, head))
    return jax.shard_map(on_device, mesh=fine, in_specs=in_specs, out_specs=out_specs, check_vma=False)
```

```python
import jax
import jax.numpy as jnp
from jax import lax
from jax.experimental import pallas as pl
from jax.experimental.pallas import tpu as pltpu
from jax.sharding import Mesh, PartitionSpec as P


DH = 64
TILE = 128
DOCS = 8
HEADS = 4
SPAN = 18
BLOCK = 90
PADDED = 96
NEG_FILL = -1e30


def attention_kernel(
    place_ref, tiles_ref, docs_ref, q_ref, own_ref, other_ref, out_ref, send_ref, slot_ref, s_ref, o_ref, b_ref, sems
):
    core = place_ref[0]
    width = HEADS * TILE

    for slot in range(tiles_ref.shape[0]):
        slot_ref[tiles_ref[slot]] = slot
    docs = docs_ref[...]
    bounds = [jnp.sum(jnp.where(docs < doc, 1.0, 0.0)).astype(jnp.int32) for doc in range(1, DOCS)]

    lane = lax.broadcasted_iota(jnp.int32, (1, TILE), 1)
    sub = lax.broadcasted_iota(jnp.int32, (2 * TILE, TILE), 0)

    def pick(tile):
        slot = slot_ref[tile]
        at = lax.shift_right_logical(slot, 1)
        return jnp.where((slot & 1) == core, own_ref[at], other_ref[at])

    copies = []
    for part in range(2):
        tile = tiles_ref[place_ref[1] + part]
        base = tile * TILE
        begin = jnp.int32(0)
        row_pos = base + lane
        row_begin = jnp.zeros((1, TILE), jnp.int32)
        for bound in bounds:
            begin = jnp.where(bound <= base, jnp.maximum(begin, bound), begin)
            row_begin = jnp.where(bound <= row_pos, jnp.maximum(row_begin, bound), row_begin)
        low = lax.div(begin, TILE)
        pairs = lax.div(tile - low + 2, 2)

        q = q_ref[part * TILE:(part + 1) * TILE, :]
        q_t = jnp.transpose(q.astype(jnp.float32) * (DH ** -0.5)).astype(jnp.bfloat16)
        q_t = jnp.concatenate([q_t[h * DH:(h + 1) * DH] for h in range(HEADS)], axis=1)
        q_t = jnp.concatenate([q_t, jnp.zeros_like(q_t)], axis=0)

        def score(pair, top):
            at = low + 2 * pair
            kv = jnp.concatenate([pick(at), pick(jnp.minimum(at + 1, tile))], axis=0)
            scores = jnp.dot(kv, q_t, preferred_element_type=jnp.float32)
            key_pos = at * TILE + sub
            allowed = (key_pos >= row_begin) & (key_pos <= row_pos)
            start = pl.multiple_of(pair * (2 * TILE), 2 * TILE)
            tops = []
            for h in range(HEADS):
                masked = jnp.where(allowed, scores[:, h * TILE:(h + 1) * TILE], NEG_FILL)
                s_ref[pl.ds(start, 2 * TILE), h * TILE:(h + 1) * TILE] = masked
                tops.append(jnp.max(masked.reshape(2 * TILE // 8, 8, TILE), axis=0))
            return jnp.maximum(top, jnp.concatenate(tops, axis=1))

        top = lax.fori_loop(0, pairs, score, jnp.full((8, width), NEG_FILL, jnp.float32))
        top = jnp.max(top, axis=0, keepdims=True)

        def add(pair, carry):
            total, summed = carry
            at = low + 2 * pair
            kv = jnp.concatenate([pick(at), pick(jnp.minimum(at + 1, tile))], axis=0)
            start = pl.multiple_of(pair * (2 * TILE), 2 * TILE)
            weights = jnp.exp(s_ref[pl.ds(start, 2 * TILE), :] - top)
            total = total + jnp.sum(weights.reshape(2 * TILE // 8, 8, width), axis=0)
            summed = summed + lax.dot_general(
                kv[:, DH:], weights.astype(jnp.bfloat16), (((0,), (0,)), ((), ())), preferred_element_type=jnp.float32
            )
            return total, summed

        total, summed = lax.fori_loop(
            0, pairs, add, (jnp.zeros((8, width), jnp.float32), jnp.zeros((DH, width), jnp.float32))
        )
        total = jnp.sum(total, axis=0, keepdims=True)
        normed = summed / total
        for h in range(0, HEADS, 2):
            both = jnp.concatenate(
                [normed[:, h * TILE:(h + 1) * TILE], normed[:, (h + 1) * TILE:(h + 2) * TILE]], axis=0
            )
            both = jnp.transpose(both)
            o_ref[part, :, h * DH:(h + 2) * DH] = both
            b_ref[part, :, h * DH:(h + 2) * DH] = both.astype(b_ref.dtype)
        rows = pl.ds(part * TILE, TILE)
        copies.append(pltpu.make_async_copy(o_ref.at[part], out_ref.at[rows], sems.at[part, 0]))
        for peer in range(send_ref.shape[0]):
            copies.append(pltpu.make_async_copy(b_ref.at[part], send_ref.at[peer, rows], sems.at[part, 1 + peer]))
        for copy in copies[-1 - send_ref.shape[0]:]:
            copy.start()
    for copy in copies:
        copy.wait()


def attention(place, tiles, docs, queries, own, other, peers):
    smem = pl.BlockSpec(memory_space=pltpu.SMEM)
    vmem = pl.BlockSpec(memory_space=pltpu.VMEM)
    rows, columns = queries.shape
    return pl.pallas_call(
        attention_kernel,
        out_shape=(
            jax.ShapeDtypeStruct((rows, columns), jnp.float32),
            jax.ShapeDtypeStruct((peers, rows, columns), jnp.bfloat16),
        ),
        in_specs=[smem, smem, vmem, vmem, vmem, vmem],
        out_specs=(pl.BlockSpec(memory_space=pl.ANY), pl.BlockSpec(memory_space=pl.ANY)),
        scratch_shapes=[
            pltpu.SMEM((tiles.shape[0],), jnp.int32),
            pltpu.VMEM((SPAN * TILE, HEADS * TILE), jnp.float32),
            pltpu.VMEM((2, TILE, columns), jnp.float32),
            pltpu.VMEM((2, TILE, columns), jnp.bfloat16),
            pltpu.SemaphoreType.DMA((2, 1 + peers)),
        ],
        cost_estimate=pl.CostEstimate(flops=1_200_000_000, bytes_accessed=4_000_000, transcendentals=2_200_000),
        compiler_params=pltpu.CompilerParams(vmem_limit_bytes=32 << 20),
    )(place, tiles, docs.reshape(-1, TILE), queries, own, other)


def term_kernel(place_ref, g00_ref, g01_ref, g10_ref, g11_ref, a_ref, own_ref, out_ref):
    core, z, x = place_ref[0], place_ref[1], place_ref[2]
    zx = lax.shift_right_logical(z, 1)
    apart = zx ^ x
    at = ((apart & 1) << 1) | lax.shift_right_logical(apart, 1)
    a = own_ref[...]
    low = (a - a.astype(jnp.bfloat16).astype(jnp.float32)).astype(jnp.bfloat16)
    for flip, sides in enumerate(((g00_ref, g01_ref), (g10_ref, g11_ref))):
        pair = (z & 1) ^ flip
        for side, g_ref in zip((core, 1 - core), sides, strict=True):
            term = jnp.dot(g_ref[at], low, preferred_element_type=jnp.float32)
            for i in range(g_ref.shape[0]):
                peer = zx ^ (((i & 1) << 1) | (i >> 1))
                term = term + jnp.dot(g_ref[i], a_ref[peer], preferred_element_type=jnp.float32)
            out_ref[2 * pair + side] = term


def term_of(place, grads, gathered, attended):
    smem = pl.BlockSpec(memory_space=pltpu.SMEM)
    vmem = pl.BlockSpec(memory_space=pltpu.VMEM)
    blocks, rows = grads[0].shape[0], grads[0].shape[1]
    return pl.pallas_call(
        term_kernel,
        out_shape=jax.ShapeDtypeStruct((blocks, rows, attended.shape[1]), jnp.float32),
        in_specs=[smem] + [vmem] * 6,
        out_specs=vmem,
        cost_estimate=pl.CostEstimate(flops=500_000_000, bytes_accessed=3_000_000, transcendentals=0),
        compiler_params=pltpu.CompilerParams(vmem_limit_bytes=32 << 20),
    )(place, *grads, gathered, attended)


def everyone(x, axes, size):
    return lax.all_to_all(jnp.broadcast_to(x[None], (size,) + x.shape), axes, 0, 0)


def on_device(queries, keys_values, grad_rows, doc_ids, tile_list):
    nx, ny, nz = (lax.axis_size(a) for a in ("x", "y", "z"))
    core, x = lax.axis_index("core"), lax.axis_index("x")
    ctx = x * ny + lax.axis_index("y")
    tokens = queries.shape[0]
    swap = [(0, 1), (1, 0)]
    half = nz // nx

    grads = jnp.pad(jnp.transpose(grad_rows).reshape(2, BLOCK, tokens), ((0, 0), (0, PADDED - BLOCK), (0, 0)))
    grads = grads.reshape(2 * PADDED, tokens)
    turn = [(a * nz + half * b + c, b * nz + half * a + c) for a in range(nx) for b in range(nx) for c in range(half)]
    home = lax.ppermute(grads, ("x", "z"), turn)
    far = lax.ppermute(grads, ("x", "z"), [(i, j ^ 4) for i, j in turn])

    mine = lax.dynamic_slice(keys_values, (core * TILE, lax.axis_index("z") * (2 * DH)), (TILE, 2 * DH))
    own = everyone(mine, "y", ny)
    own = everyone(own, "x", nx).reshape(nx * ny, TILE, 2 * DH)
    other = lax.ppermute(own, "core", swap)

    g_own = jnp.stack([home, far])
    came = lax.ppermute(g_own, "z", [(i, i ^ 2) for i in range(nz)])
    g_own = jnp.concatenate([g_own, came], axis=0)
    g_next = lax.ppermute(g_own, "z", [(i, i ^ 1) for i in range(nz)])
    g_other = lax.ppermute(g_own, "core", swap)
    g_both = lax.ppermute(g_next, "core", swap)

    place = jnp.stack([core, 2 * ctx])
    attended, send = attention(place, tile_list, doc_ids, queries, own, other, nx)
    gathered = lax.all_to_all(send, "x", 0, 0)
    place = jnp.stack([core, lax.axis_index("z"), x])
    term = term_of(place, (g_own, g_other, g_next, g_both), gathered, attended)
    parts = lax.all_to_all(term.reshape(ny, PADDED, -1), "y", 0, 0)
    weight_grad = jnp.sum(parts, axis=0)[:BLOCK]
    return attended, weight_grad


def solution(mesh):
    fine = Mesh(mesh.devices.reshape(4, 8, 8, 2), ("x", "y", "z", "core"))
    ctx, head = ("x", "y"), ("z", "core")
    in_specs = (P(ctx, head), P(ctx, None), P(ctx, head), P(), P())
    out_specs = (P(ctx, head), P(ctx, head))
    return jax.shard_map(on_device, mesh=fine, in_specs=in_specs, out_specs=out_specs, check_vma=False)
```

```python
import jax
import jax.numpy as jnp
from jax import lax
from jax.experimental import pallas as pl
from jax.experimental.pallas import tpu as pltpu
from jax.sharding import Mesh, PartitionSpec as P


DH = 64
TILE = 128
DOCS = 8
HEADS = 4
SPAN = 18
BLOCK = 90
PADDED = 96
NEG_FILL = -1e30


def attention_kernel(
    place_ref, tiles_ref, docs_ref, q_ref, own_ref, other_ref, out_ref, send_ref, slot_ref, s_ref, o_ref, sems
):
    core = place_ref[0]
    width = HEADS * TILE

    for slot in range(tiles_ref.shape[0]):
        slot_ref[tiles_ref[slot]] = slot
    docs = docs_ref[...]
    bounds = [jnp.sum(jnp.where(docs < doc, 1.0, 0.0)).astype(jnp.int32) for doc in range(1, DOCS)]

    lane = lax.broadcasted_iota(jnp.int32, (1, TILE), 1)
    sub = lax.broadcasted_iota(jnp.int32, (2 * TILE, TILE), 0)

    def pick(tile):
        slot = slot_ref[tile]
        at = lax.shift_right_logical(slot, 1)
        return jnp.where((slot & 1) == core, own_ref[at], other_ref[at])

    copies = []
    for part in range(2):
        tile = tiles_ref[place_ref[1] + part]
        base = tile * TILE
        begin = jnp.int32(0)
        row_pos = base + lane
        row_begin = jnp.zeros((1, TILE), jnp.int32)
        for bound in bounds:
            begin = jnp.where(bound <= base, jnp.maximum(begin, bound), begin)
            row_begin = jnp.where(bound <= row_pos, jnp.maximum(row_begin, bound), row_begin)
        low = lax.div(begin, TILE)
        pairs = lax.div(tile - low + 2, 2)

        q = q_ref[part * TILE:(part + 1) * TILE, :]
        q_t = jnp.transpose(q.astype(jnp.float32) * (DH ** -0.5)).astype(jnp.bfloat16)
        q_t = jnp.concatenate([q_t[h * DH:(h + 1) * DH] for h in range(HEADS)], axis=1)
        q_t = jnp.concatenate([q_t, jnp.zeros_like(q_t)], axis=0)

        def score(pair, top):
            at = low + 2 * pair
            kv = jnp.concatenate([pick(at), pick(jnp.minimum(at + 1, tile))], axis=0)
            scores = jnp.dot(kv, q_t, preferred_element_type=jnp.float32)
            key_pos = at * TILE + sub
            allowed = (key_pos >= row_begin) & (key_pos <= row_pos)
            start = pl.multiple_of(pair * (2 * TILE), 2 * TILE)
            tops = []
            for h in range(HEADS):
                masked = jnp.where(allowed, scores[:, h * TILE:(h + 1) * TILE], NEG_FILL)
                s_ref[pl.ds(start, 2 * TILE), h * TILE:(h + 1) * TILE] = masked
                tops.append(jnp.max(masked.reshape(2 * TILE // 8, 8, TILE), axis=0))
            return jnp.maximum(top, jnp.concatenate(tops, axis=1))

        top = lax.fori_loop(0, pairs, score, jnp.full((8, width), NEG_FILL, jnp.float32))
        top = jnp.max(top, axis=0, keepdims=True)

        def add(pair, carry):
            total, summed = carry
            at = low + 2 * pair
            kv = jnp.concatenate([pick(at), pick(jnp.minimum(at + 1, tile))], axis=0)
            start = pl.multiple_of(pair * (2 * TILE), 2 * TILE)
            weights = jnp.exp(s_ref[pl.ds(start, 2 * TILE), :] - top)
            total = total + jnp.sum(weights.reshape(2 * TILE // 8, 8, width), axis=0)
            summed = summed + lax.dot_general(
                kv[:, DH:], weights.astype(jnp.bfloat16), (((0,), (0,)), ((), ())), preferred_element_type=jnp.float32
            )
            return total, summed

        total, summed = lax.fori_loop(
            0, pairs, add, (jnp.zeros((8, width), jnp.float32), jnp.zeros((DH, width), jnp.float32))
        )
        total = jnp.sum(total, axis=0, keepdims=True)
        normed = summed / total
        for h in range(0, HEADS, 2):
            both = jnp.concatenate(
                [normed[:, h * TILE:(h + 1) * TILE], normed[:, (h + 1) * TILE:(h + 2) * TILE]], axis=0
            )
            both = jnp.transpose(both)
            o_ref[part, :, h * DH:(h + 2) * DH] = both
        rows = pl.ds(part * TILE, TILE)
        copies.append(pltpu.make_async_copy(o_ref.at[part], out_ref.at[rows], sems.at[part, 0]))
        for peer in range(send_ref.shape[0]):
            copies.append(pltpu.make_async_copy(o_ref.at[part], send_ref.at[peer, rows], sems.at[part, 1 + peer]))
        for copy in copies[-1 - send_ref.shape[0]:]:
            copy.start()
    for copy in copies:
        copy.wait()


def attention(place, tiles, docs, queries, own, other, peers):
    smem = pl.BlockSpec(memory_space=pltpu.SMEM)
    vmem = pl.BlockSpec(memory_space=pltpu.VMEM)
    rows, columns = queries.shape
    return pl.pallas_call(
        attention_kernel,
        out_shape=(
            jax.ShapeDtypeStruct((rows, columns), jnp.float32),
            jax.ShapeDtypeStruct((peers, rows, columns), jnp.float32),
        ),
        in_specs=[smem, smem, vmem, vmem, vmem, vmem],
        out_specs=(pl.BlockSpec(memory_space=pl.ANY), pl.BlockSpec(memory_space=pl.ANY)),
        scratch_shapes=[
            pltpu.SMEM((tiles.shape[0],), jnp.int32),
            pltpu.VMEM((SPAN * TILE, HEADS * TILE), jnp.float32),
            pltpu.VMEM((2, TILE, columns), jnp.float32),
            pltpu.SemaphoreType.DMA((2, 1 + peers)),
        ],
        cost_estimate=pl.CostEstimate(flops=1_200_000_000, bytes_accessed=4_000_000, transcendentals=2_200_000),
        compiler_params=pltpu.CompilerParams(vmem_limit_bytes=32 << 20),
    )(place, tiles, docs.reshape(-1, TILE), queries, own, other)


def term_kernel(place_ref, g00_ref, g01_ref, g10_ref, g11_ref, a_ref, out_ref, own_ref, high_ref, low_ref, sum_ref):
    core, z, y = place_ref[0], place_ref[1], place_ref[2]
    a = a_ref[...]
    high = a.astype(jnp.bfloat16)
    high_ref[...] = high
    low_ref[...] = (a - high.astype(jnp.float32)).astype(jnp.bfloat16)
    for flip, sides in enumerate(((g00_ref, g01_ref), (g10_ref, g11_ref))):
        pair = (z & 1) ^ flip
        for side, g_ref in zip((core, 1 - core), sides, strict=True):
            term = None
            for i in range(g_ref.shape[0]):
                peer = lax.shift_right_logical(z, 1) ^ (((i & 1) << 1) | (i >> 1))
                for half_ref in (high_ref, low_ref):
                    part = jnp.dot(g_ref[i], half_ref[peer], preferred_element_type=jnp.float32)
                    term = part if term is None else term + part
            sum_ref[2 * pair + side] = term
            out_ref[2 * pair + side] = term.astype(out_ref.dtype)
    own_ref[...] = sum_ref[lax.shift_right_logical(y, 1), pl.ds(pl.multiple_of((y & 1) * PADDED, PADDED), PADDED), :]


def term_of(place, grads, gathered):
    smem = pl.BlockSpec(memory_space=pltpu.SMEM)
    vmem = pl.BlockSpec(memory_space=pltpu.VMEM)
    blocks, rows = grads[0].shape[0], grads[0].shape[1]
    columns = gathered.shape[2]
    return pl.pallas_call(
        term_kernel,
        out_shape=(
            jax.ShapeDtypeStruct((blocks, rows, columns), jnp.bfloat16),
            jax.ShapeDtypeStruct((PADDED, columns), jnp.float32),
        ),
        in_specs=[smem] + [vmem] * 5,
        out_specs=(vmem, vmem),
        scratch_shapes=[
            pltpu.VMEM(gathered.shape, jnp.bfloat16),
            pltpu.VMEM(gathered.shape, jnp.bfloat16),
            pltpu.VMEM((blocks, rows, columns), jnp.float32),
        ],
        cost_estimate=pl.CostEstimate(flops=900_000_000, bytes_accessed=3_000_000, transcendentals=0),
        compiler_params=pltpu.CompilerParams(vmem_limit_bytes=32 << 20),
    )(place, *grads, gathered)


def everyone(x, axes, size):
    return lax.all_to_all(jnp.broadcast_to(x[None], (size,) + x.shape), axes, 0, 0)


def on_device(queries, keys_values, grad_rows, doc_ids, tile_list):
    nx, ny, nz = (lax.axis_size(a) for a in ("x", "y", "z"))
    core, x = lax.axis_index("core"), lax.axis_index("x")
    ctx = x * ny + lax.axis_index("y")
    tokens = queries.shape[0]
    swap = [(0, 1), (1, 0)]
    half = nz // nx

    grads = jnp.pad(jnp.transpose(grad_rows).reshape(2, BLOCK, tokens), ((0, 0), (0, PADDED - BLOCK), (0, 0)))
    grads = grads.reshape(2 * PADDED, tokens)
    turn = [(a * nz + half * b + c, b * nz + half * a + c) for a in range(nx) for b in range(nx) for c in range(half)]
    home = lax.ppermute(grads, ("x", "z"), turn)
    far = lax.ppermute(grads, ("x", "z"), [(i, j ^ 4) for i, j in turn])

    mine = lax.dynamic_slice(keys_values, (core * TILE, lax.axis_index("z") * (2 * DH)), (TILE, 2 * DH))
    own = everyone(mine, "y", ny)
    own = everyone(own, "x", nx).reshape(nx * ny, TILE, 2 * DH)
    other = lax.ppermute(own, "core", swap)

    g_own = jnp.stack([home, far])
    came = lax.ppermute(g_own, "z", [(i, i ^ 2) for i in range(nz)])
    g_own = jnp.concatenate([g_own, came], axis=0)
    g_next = lax.ppermute(g_own, "z", [(i, i ^ 1) for i in range(nz)])
    g_other = lax.ppermute(g_own, "core", swap)
    g_both = lax.ppermute(g_next, "core", swap)

    place = jnp.stack([core, 2 * ctx])
    attended, send = attention(place, tile_list, doc_ids, queries, own, other, nx)
    gathered = lax.all_to_all(send, "x", 0, 0)
    y = lax.axis_index("y")
    place = jnp.stack([core, lax.axis_index("z"), y])
    term, mine = term_of(place, (g_own, g_other, g_next, g_both), gathered)
    parts = lax.all_to_all(term.reshape(ny, PADDED, -1), "y", 0, 0)
    others = lax.broadcasted_iota(jnp.int32, parts.shape, 0) != y
    weight_grad = (mine + jnp.sum(jnp.where(others, parts.astype(jnp.float32), 0.0), axis=0))[:BLOCK]
    return attended, weight_grad


def solution(mesh):
    fine = Mesh(mesh.devices.reshape(4, 8, 8, 2), ("x", "y", "z", "core"))
    ctx, head = ("x", "y"), ("z", "core")
    in_specs = (P(ctx, head), P(ctx, None), P(ctx, head), P(), P())
    out_specs = (P(ctx, head), P(ctx, head))
    return jax.shard_map(on_device, mesh=fine, in_specs=in_specs, out_specs=out_specs, check_vma=False)
```

```python
import jax
import jax.numpy as jnp
from jax import lax
from jax.experimental import pallas as pl
from jax.experimental.pallas import tpu as pltpu
from jax.sharding import Mesh, PartitionSpec as P


DH = 64
TILE = 128
DOCS = 8
HEADS = 4
SPAN = 18
BLOCK = 90
PADDED = 96
NEG_FILL = -1e30


def attention_kernel(
    place_ref, tiles_ref, docs_ref, q_ref, own_ref, other_ref, out_ref, send_ref, slot_ref, s_ref, o_ref, sems
):
    core = place_ref[0]
    width = HEADS * TILE

    for slot in range(tiles_ref.shape[0]):
        slot_ref[tiles_ref[slot]] = slot
    docs = docs_ref[...]
    bounds = [jnp.sum(jnp.where(docs < doc, 1.0, 0.0)).astype(jnp.int32) for doc in range(1, DOCS)]

    lane = lax.broadcasted_iota(jnp.int32, (1, TILE), 1)
    sub = lax.broadcasted_iota(jnp.int32, (2 * TILE, TILE), 0)

    def pick(tile):
        slot = slot_ref[tile]
        at = lax.shift_right_logical(slot, 1)
        return jnp.where((slot & 1) == core, own_ref[at], other_ref[at])

    copies = []
    for part in range(2):
        tile = tiles_ref[place_ref[1] + part]
        base = tile * TILE
        begin = jnp.int32(0)
        row_pos = base + lane
        row_begin = jnp.zeros((1, TILE), jnp.int32)
        for bound in bounds:
            begin = jnp.where(bound <= base, jnp.maximum(begin, bound), begin)
            row_begin = jnp.where(bound <= row_pos, jnp.maximum(row_begin, bound), row_begin)
        low = lax.div(begin, TILE)
        pairs = lax.div(tile - low + 2, 2)

        q = q_ref[part * TILE:(part + 1) * TILE, :]
        q_t = jnp.transpose(q.astype(jnp.float32) * (DH ** -0.5)).astype(jnp.bfloat16)
        q_t = jnp.concatenate([q_t[h * DH:(h + 1) * DH] for h in range(HEADS)], axis=1)
        q_t = jnp.concatenate([q_t, jnp.zeros_like(q_t)], axis=0)

        def score(pair, top):
            at = low + 2 * pair
            kv = jnp.concatenate([pick(at), pick(jnp.minimum(at + 1, tile))], axis=0)
            scores = jnp.dot(kv, q_t, preferred_element_type=jnp.float32)
            allowed = (sub >= row_begin - at * TILE) & (sub <= row_pos - at * TILE)
            start = pl.multiple_of(pair * (2 * TILE), 2 * TILE)
            tops = []
            for h in range(HEADS):
                masked = jnp.where(allowed, scores[:, h * TILE:(h + 1) * TILE], NEG_FILL)
                s_ref[pl.ds(start, 2 * TILE), h * TILE:(h + 1) * TILE] = masked
                tops.append(jnp.max(masked.reshape(2 * TILE // 8, 8, TILE), axis=0))
            return jnp.maximum(top, jnp.concatenate(tops, axis=1))

        top = lax.fori_loop(0, pairs, score, jnp.full((8, width), NEG_FILL, jnp.float32))
        top = jnp.max(top, axis=0, keepdims=True)

        def add(pair, carry):
            total, summed = carry
            at = low + 2 * pair
            kv = jnp.concatenate([pick(at), pick(jnp.minimum(at + 1, tile))], axis=0)
            start = pl.multiple_of(pair * (2 * TILE), 2 * TILE)
            weights = jnp.exp(s_ref[pl.ds(start, 2 * TILE), :] - top)
            total = total + jnp.sum(weights.reshape(2 * TILE // 8, 8, width), axis=0)
            summed = summed + lax.dot_general(
                kv[:, DH:], weights.astype(jnp.bfloat16), (((0,), (0,)), ((), ())), preferred_element_type=jnp.float32
            )
            return total, summed

        total, summed = lax.fori_loop(
            0, pairs, add, (jnp.zeros((8, width), jnp.float32), jnp.zeros((DH, width), jnp.float32))
        )
        total = jnp.sum(total, axis=0, keepdims=True)
        normed = summed / total
        for h in range(0, HEADS, 2):
            both = jnp.concatenate(
                [normed[:, h * TILE:(h + 1) * TILE], normed[:, (h + 1) * TILE:(h + 2) * TILE]], axis=0
            )
            both = jnp.transpose(both)
            o_ref[part, :, h * DH:(h + 2) * DH] = both
        rows = pl.ds(part * TILE, TILE)
        copies.append(pltpu.make_async_copy(o_ref.at[part], out_ref.at[rows], sems.at[part, 0]))
        for peer in range(send_ref.shape[0]):
            copies.append(pltpu.make_async_copy(o_ref.at[part], send_ref.at[peer, rows], sems.at[part, 1 + peer]))
        for copy in copies[-1 - send_ref.shape[0]:]:
            copy.start()
    for copy in copies:
        copy.wait()


def attention(place, tiles, docs, queries, own, other, peers):
    smem = pl.BlockSpec(memory_space=pltpu.SMEM)
    vmem = pl.BlockSpec(memory_space=pltpu.VMEM)
    rows, columns = queries.shape
    return pl.pallas_call(
        attention_kernel,
        out_shape=(
            jax.ShapeDtypeStruct((rows, columns), jnp.float32),
            jax.ShapeDtypeStruct((peers, rows, columns), jnp.float32),
        ),
        in_specs=[smem, smem, vmem, vmem, vmem, vmem],
        out_specs=(pl.BlockSpec(memory_space=pl.ANY), pl.BlockSpec(memory_space=pl.ANY)),
        scratch_shapes=[
            pltpu.SMEM((tiles.shape[0],), jnp.int32),
            pltpu.VMEM((SPAN * TILE, HEADS * TILE), jnp.float32),
            pltpu.VMEM((2, TILE, columns), jnp.float32),
            pltpu.SemaphoreType.DMA((2, 1 + peers)),
        ],
        cost_estimate=pl.CostEstimate(flops=1_200_000_000, bytes_accessed=4_000_000, transcendentals=2_200_000),
        compiler_params=pltpu.CompilerParams(vmem_limit_bytes=32 << 20),
    )(place, tiles, docs.reshape(-1, TILE), queries, own, other)


def term_kernel(place_ref, g00_ref, g01_ref, g10_ref, g11_ref, a_ref, out_ref, own_ref, high_ref, low_ref, sum_ref):
    core, z, y = place_ref[0], place_ref[1], place_ref[2]
    a = a_ref[...]
    high = a.astype(jnp.bfloat16)
    high_ref[...] = high
    low_ref[...] = (a - high.astype(jnp.float32)).astype(jnp.bfloat16)
    for flip, sides in enumerate(((g00_ref, g01_ref), (g10_ref, g11_ref))):
        pair = (z & 1) ^ flip
        for side, g_ref in zip((core, 1 - core), sides, strict=True):
            term = None
            for i in range(g_ref.shape[0]):
                peer = lax.shift_right_logical(z, 1) ^ (((i & 1) << 1) | (i >> 1))
                for half_ref in (high_ref, low_ref):
                    part = jnp.dot(g_ref[i], half_ref[peer], preferred_element_type=jnp.float32)
                    term = part if term is None else term + part
            sum_ref[2 * pair + side] = term
            out_ref[2 * pair + side] = term.astype(out_ref.dtype)
    own_ref[...] = sum_ref[lax.shift_right_logical(y, 1), pl.ds(pl.multiple_of((y & 1) * PADDED, PADDED), PADDED), :]


def term_of(place, grads, gathered):
    smem = pl.BlockSpec(memory_space=pltpu.SMEM)
    vmem = pl.BlockSpec(memory_space=pltpu.VMEM)
    blocks, rows = grads[0].shape[0], grads[0].shape[1]
    columns = gathered.shape[2]
    return pl.pallas_call(
        term_kernel,
        out_shape=(
            jax.ShapeDtypeStruct((blocks, rows, columns), jnp.bfloat16),
            jax.ShapeDtypeStruct((PADDED, columns), jnp.float32),
        ),
        in_specs=[smem] + [vmem] * 5,
        out_specs=(vmem, vmem),
        scratch_shapes=[
            pltpu.VMEM(gathered.shape, jnp.bfloat16),
            pltpu.VMEM(gathered.shape, jnp.bfloat16),
            pltpu.VMEM((blocks, rows, columns), jnp.float32),
        ],
        cost_estimate=pl.CostEstimate(flops=900_000_000, bytes_accessed=3_000_000, transcendentals=0),
        compiler_params=pltpu.CompilerParams(vmem_limit_bytes=32 << 20),
    )(place, *grads, gathered)


def everyone(x, axes, size):
    return lax.all_to_all(jnp.broadcast_to(x[None], (size,) + x.shape), axes, 0, 0)


def on_device(queries, keys_values, grad_rows, doc_ids, tile_list):
    nx, ny, nz = (lax.axis_size(a) for a in ("x", "y", "z"))
    core, x = lax.axis_index("core"), lax.axis_index("x")
    ctx = x * ny + lax.axis_index("y")
    tokens = queries.shape[0]
    swap = [(0, 1), (1, 0)]
    half = nz // nx

    grads = jnp.pad(jnp.transpose(grad_rows).reshape(2, BLOCK, tokens), ((0, 0), (0, PADDED - BLOCK), (0, 0)))
    grads = grads.reshape(2 * PADDED, tokens)
    turn = [(a * nz + half * b + c, b * nz + half * a + c) for a in range(nx) for b in range(nx) for c in range(half)]
    home = lax.ppermute(grads, ("x", "z"), turn)
    far = lax.ppermute(grads, ("x", "z"), [(i, j ^ 4) for i, j in turn])

    mine = lax.dynamic_slice(keys_values, (core * TILE, lax.axis_index("z") * (2 * DH)), (TILE, 2 * DH))
    own = everyone(mine, "y", ny)
    own = everyone(own, "x", nx).reshape(nx * ny, TILE, 2 * DH)
    other = lax.ppermute(own, "core", swap)

    g_own = jnp.stack([home, far])
    came = lax.ppermute(g_own, "z", [(i, i ^ 2) for i in range(nz)])
    g_own = jnp.concatenate([g_own, came], axis=0)
    g_next = lax.ppermute(g_own, "z", [(i, i ^ 1) for i in range(nz)])
    g_other = lax.ppermute(g_own, "core", swap)
    g_both = lax.ppermute(g_next, "core", swap)

    place = jnp.stack([core, 2 * ctx])
    attended, send = attention(place, tile_list, doc_ids, queries, own, other, nx)
    gathered = lax.all_to_all(send, "x", 0, 0)
    y = lax.axis_index("y")
    place = jnp.stack([core, lax.axis_index("z"), y])
    term, mine = term_of(place, (g_own, g_other, g_next, g_both), gathered)
    parts = lax.all_to_all(term.reshape(ny, PADDED, -1), "y", 0, 0)
    parts = parts[:, :BLOCK]
    others = lax.broadcasted_iota(jnp.int32, parts.shape, 0) != y
    weight_grad = mine[:BLOCK] + jnp.sum(jnp.where(others, parts.astype(jnp.float32), 0.0), axis=0)
    return attended, weight_grad


def solution(mesh):
    fine = Mesh(mesh.devices.reshape(4, 8, 8, 2), ("x", "y", "z", "core"))
    ctx, head = ("x", "y"), ("z", "core")
    in_specs = (P(ctx, head), P(ctx, None), P(ctx, head), P(), P())
    out_specs = (P(ctx, head), P(ctx, head))
    return jax.shard_map(on_device, mesh=fine, in_specs=in_specs, out_specs=out_specs, check_vma=False)
```
